512 devices in a mesh: gx: 32 (over z, x), gy: 16 (over y, core).
Axes of the slice: x: 4, y: 8, z: 8, core: 2. Of those that a mesh axis runs over, the one named last changes fastest.
Arguments:
- probe_seeds: int32 [4], replicated, may hold values from 0 to 1048575
- damping: float32 [2048, 4096], P('gx', 'gy'), may hold values from 0.2 to 1
- coupling_x: float32 [2048, 4096], P('gx', 'gy'), may hold values from 0.05 to 0.5
- coupling_y: float32 [2048, 4096], P('gx', 'gy'), may hold values from 0.05 to 0.5
- sensor_count: int32 [32, 16], P('gx', 'gy'), may hold values from 1 to 256, as said below
- sensor_cells: int32 [32, 16, 256], P('gx', 'gy'), may hold values from 0 to 16383
- obs_weight: float32 [32, 16, 256, 256], P('gx', 'gy'), as said below
Outputs:
- solution: float32 [4, 2048, 4096], P(None, 'gx', 'gy')
- trace_estimate: float32 [], replicated
The draws below stay inside these ranges and needn't reach their ends.
Inputs may be any that keep to these rules, and one draw needn't show every extreme that they name: `sensor_count`: at most 256, and some block has exactly 256 in every draw; blocks near a few cluster centres are far busier than the rest. `sensor_cells`: cells within the block, numbered row by row. `obs_weight`: each block's matrix is symmetric positive definite.
All inputs are finite; a program needn't handle non-finite values.
Results may differ from the reference program's by a relative error of at most 0.0003.
Values sent between devices are 32-bit elements; how exact they have to be, the bound alone decides.
A program may use at most 64 MiB of HBM per device.

```python
import math
import jax
import jax.numpy as jnp
from jax import lax

PROBES = 4
CX = 64
CY = 256
SMAX = 256
BX = 32
BY = 16
NX = 2048
NY = 4096


def draw_sensor_count(key, part):
    key_base, key_rows, key_cols = jax.random.split(jax.random.fold_in(key, 101), 3)
    base = jax.random.randint(key_base, (BX, BY), 1, SMAX // 4 + 1)
    centre_rows = jax.random.randint(key_rows, (3,), 0, BX)
    centre_cols = jax.random.randint(key_cols, (3,), 0, BY)
    block_rows = jnp.arange(BX, dtype=jnp.int32)[:, None, None]
    block_cols = jnp.arange(BY, dtype=jnp.int32)[None, :, None]
    apart_rows = jnp.abs(block_rows - centre_rows[None, None, :])
    apart_rows = jnp.minimum(apart_rows, BX - apart_rows)
    apart_cols = jnp.abs(block_cols - centre_cols[None, None, :])
    apart_cols = jnp.minimum(apart_cols, BY - apart_cols)
    distance = apart_rows + apart_cols
    centre = jnp.any(distance == 0, axis=2)
    nearby = jnp.any(distance <= 1, axis=2)
    counts = jnp.where(nearby, jnp.maximum(base, SMAX // 2), base)
    return jnp.where(centre, SMAX, counts).astype(jnp.int32)


def draw_obs_weight(key, part):
    key_mix, key_diag = jax.random.split(jax.random.fold_in(key, 202))
    normal_part = jax.random.normal(key_mix, (BX, BY, SMAX, SMAX), jnp.float32)
    product = jnp.einsum('abij,abkj->abik', normal_part, normal_part) / (2.0 * math.sqrt(SMAX))
    product = 0.5 * (product + jnp.swapaxes(product, 2, 3))
    diagonal = jnp.exp(jax.random.uniform(key_diag, (BX, BY, SMAX), jnp.float32, 0.0, math.log(10.0)))
    return (product + diagonal[..., None] * jnp.eye(SMAX, dtype=jnp.float32)).astype(jnp.float32)


def touch_ends(result, own_key, smallest, top_value):
    index_at = [jax.random.randint(jax.random.fold_in(own_key, axis), (), 0, length) for axis, length in enumerate(result.shape)]
    widest = result.shape.index(max(result.shape))
    next_to = index_at[:widest] + [(index_at[widest] + 1) % result.shape[widest]] + index_at[widest + 1:]
    return result.at[tuple(index_at)].set(smallest).at[tuple(next_to)].set(top_value)


def shard_levels(key, shape, shards, least, high):
    def one(axis_at, parts):
        heights = jax.random.uniform(jax.random.fold_in(jax.random.fold_in(key, 6), axis_at), (parts,), jnp.float32, least / len(shards), high / len(shards))
        return jnp.repeat(jnp.exp(heights), shape[axis_at] // parts).reshape((-1,) + (1,) * (len(shape) - axis_at - 1))

    gain = one(*shards[0])
    for cut in shards[1:]:
        gain = gain * one(*cut)
    return gain


def setup_inputs(seed: int = 0) -> dict:
    key_list = jax.random.split(jax.random.key(seed), 8)
    probe_seeds = touch_ends(jax.random.randint(key_list[0], (PROBES,), 0, 1048576), jax.random.fold_in(key_list[0], 1), 0, 1048575).astype(jnp.int32)
    damping = jnp.clip(jnp.exp(math.log(1.0) - 1.609438 * jax.random.uniform(key_list[1], (NX, NY), jnp.float32) ** shard_levels(key_list[1], (NX, NY), ((0, 32), (1, 16)), -0.2, 0.2)), 0.2, 1.0)
    coupling_x = jnp.clip(jnp.exp(math.log(0.5) - 2.3025851 * jax.random.uniform(key_list[2], (NX, NY), jnp.float32) ** shard_levels(key_list[2], (NX, NY), ((0, 32), (1, 16)), -0.2, 0.2)), 0.05, 0.5)
    coupling_y = jnp.clip(jnp.exp(math.log(0.5) - 2.3025851 * jax.random.uniform(key_list[3], (NX, NY), jnp.float32) ** shard_levels(key_list[3], (NX, NY), ((0, 32), (1, 16)), -0.2, 0.2)), 0.05, 0.5)
    sensor_count = draw_sensor_count(jax.random.fold_in(key_list[7], 71), 0)
    sensor_cells = touch_ends(jax.random.randint(key_list[5], (BX, BY, SMAX), 0, CX * CY), jax.random.fold_in(key_list[5], 1), 0, (CX * CY) - 1).astype(jnp.int32)
    obs_weight = draw_obs_weight(jax.random.fold_in(key_list[7], 71), 0)
    return dict(probe_seeds=probe_seeds, damping=damping, coupling_x=coupling_x, coupling_y=coupling_y, sensor_count=sensor_count, sensor_cells=sensor_cells, obs_weight=obs_weight)


probe_block = 4


def rademacher(seeds, row_ids, col_ids):
    mixed = seeds[:, None, None] * 668265261 + row_ids[None, :, None] * 374761393 + col_ids[None, None, :] * 1103515245
    mixed = (mixed ^ ((mixed >> 16) & 65535)) * 73244475
    mixed = (mixed ^ ((mixed >> 16) & 65535)) * 73244475
    mixed = mixed ^ ((mixed >> 16) & 65535)
    bit_value = (mixed >> 7) & 1
    return (2 * bit_value - 1).astype(jnp.float32)


def apply_operator(field, damping, coupling_x, coupling_y):
    below = jnp.roll(field, -1, 1)
    above = jnp.roll(field, 1, 1)
    right = jnp.roll(field, -1, 2)
    left_side = jnp.roll(field, 1, 2)
    return (damping * field + coupling_x * (field - below) + jnp.roll(coupling_x, 1, 0) * (field - above)
            + coupling_y * (field - right) + jnp.roll(coupling_y, 1, 1) * (field - left_side))


def observe_block(field, count, cell_ids, weight):
    mask = (jnp.arange(SMAX) < count).astype(field.dtype)
    sampled = field[:, cell_ids] * mask
    weighted = jnp.dot(sampled, weight, precision=lax.Precision.HIGHEST) * mask
    return jnp.zeros_like(field).at[:, cell_ids].add(weighted)


def observe(field, sensor_count, sensor_cells, obs_weight):
    group = field.shape[0]
    blocks = field.reshape(group, BX, CX, BY, CY).transpose(1, 3, 0, 2, 4).reshape(BX * BY, group, CX * CY)
    added = jax.vmap(observe_block)(blocks, sensor_count.reshape(-1), sensor_cells.reshape(-1, SMAX),
                                    obs_weight.reshape(-1, SMAX, SMAX))
    return added.reshape(BX, BY, group, CX, CY).transpose(2, 0, 3, 1, 4).reshape(group, NX, NY)


def reference(probe_seeds, damping, coupling_x, coupling_y, sensor_count, sensor_cells, obs_weight):
    row_ids = jnp.arange(NX, dtype=jnp.int32)
    col_ids = jnp.arange(NY, dtype=jnp.int32)

    def hessian(field):
        once = apply_operator(field, damping, coupling_x, coupling_y)
        twice = apply_operator(once, damping, coupling_x, coupling_y)
        return twice + observe(field, sensor_count, sensor_cells, obs_weight)

    def solve_group(seeds):
        probes = rademacher(seeds, row_ids, col_ids)
        norm_start = jnp.sum(probes * probes, axis=(1, 2))
        image = hessian(probes)
        first_step = norm_start / jnp.sum(probes * image, axis=(1, 2))
        solution = first_step[:, None, None] * probes
        residual = probes - first_step[:, None, None] * image
        norm_next = jnp.sum(residual * residual, axis=(1, 2))
        direction = residual + (norm_next / norm_start)[:, None, None] * probes
        image = hessian(direction)
        second_step = norm_next / jnp.sum(direction * image, axis=(1, 2))
        solution = solution + second_step[:, None, None] * direction
        return solution, jnp.sum(probes * solution, axis=(1, 2))

    solutions, products = lax.map(solve_group, probe_seeds.reshape(-1, probe_block))
    return solutions.reshape(PROBES, NX, NY), jnp.sum(products) / PROBES
```

```python
import jax
import jax.numpy as jnp
from jax import lax
from jax.experimental import pallas as pl
from jax.experimental.pallas import tpu as pltpu
from jax.sharding import PartitionSpec as P

MESH = pl.DeviceIdType.MESH
NT = (((1,), (1,)), ((), ()))
F32 = jnp.float32
BF16 = jnp.bfloat16

PAD_R, PAD_C = 8, 128


def mix(base):
    mixed = (base ^ ((base >> 16) & 65535)) * 73244475
    mixed = (mixed ^ ((mixed >> 16) & 65535)) * 73244475
    mixed = mixed ^ ((mixed >> 16) & 65535)
    return (2 * ((mixed >> 7) & 1) - 1).astype(F32)


def position(rows, cols):
    return rows * 374761393 + cols * 1103515245


def iota(shape, dim):
    return lax.broadcasted_iota(jnp.int32, shape, dim)


def split3(x):
    high = x.astype(BF16)
    rest = x - high.astype(F32)
    mid = rest.astype(BF16)
    low = (rest - mid.astype(F32)).astype(BF16)
    return high, mid, low


def times(x, y, dims=(((1,), (0,)), ((), ()))):
    total = None
    for part in reversed(split3(x)):
        one = lax.dot_general(part, y, dims, preferred_element_type=F32)
        total = one if total is None else total + one
    return total


def kernel_of(probes, bx, by, rows, cols):
    ext_r, ext_c = rows + 2 * PAD_R, cols + 2 * PAD_C
    nx, ny = bx * rows, by * cols
    r_in = slice(PAD_R, PAD_R + rows)
    c_in = slice(PAD_C, PAD_C + cols)
    first_r, last_r = slice(PAD_R, 2 * PAD_R), slice(rows, PAD_R + rows)
    first_c, last_c = slice(PAD_C, 2 * PAD_C), slice(cols, PAD_C + cols)
    halo_r = {-1: slice(0, PAD_R), 0: r_in, 1: slice(PAD_R + rows, ext_r)}
    halo_c = {-1: slice(0, PAD_C), 0: c_in, 1: slice(PAD_C + cols, ext_c)}
    edge_r = {-1: first_r, 0: r_in, 1: last_r}
    edge_c = {-1: first_c, 0: c_in, 1: last_c}
    near = [(a, b) for a in (-1, 0, 1) for b in (-1, 0, 1) if (a, b) != (0, 0)]
    cross = [(0, 1), (0, -1), (1, 0), (-1, 0)]
    corners = [(a, b) for a in (-1, 1) for b in (-1, 1)]

    def body(seeds_h, damp_h, cx_h, cy_h, count_h, cells_h, weight_h, sol_ref, trace_ref,
             seeds_s, count_s, cells_v, weight_v, coef, up_v, left_v, diag_v, prob, once, image,
             w_send, w_recv, part, got_y, got_x,
             local_sem, coef_send, coef_recv, obs_send, obs_recv, y_send, y_recv, x_send, x_recv):
        gx, gy = lax.axis_index("gx"), lax.axis_index("gy")

        def at(dx, dy):
            return (lax.rem(gx + (dx + bx), bx), lax.rem(gy + (dy + by), by))

        barrier = pltpu.get_barrier_semaphore()
        peers = [(0, d) for d in range(1, by)] + [(d, 0) for d in range(1, bx)] + corners
        for dx, dy in cross + corners:
            pl.semaphore_signal(barrier, inc=1, device_id=at(dx, dy), device_id_type=MESH)
        for dx, dy in peers:
            if (dx, dy) not in corners and (dx, dy) not in ((0, 1), (0, by - 1), (1, 0), (bx - 1, 0)):
                pl.semaphore_signal(barrier, inc=1, device_id=at(dx, dy), device_id_type=MESH)

        loads = [
            pltpu.make_async_copy(damp_h, coef.at[0, r_in, c_in], local_sem.at[0]),
            pltpu.make_async_copy(cx_h, coef.at[1, r_in, c_in], local_sem.at[1]),
            pltpu.make_async_copy(cy_h, coef.at[2, r_in, c_in], local_sem.at[2]),
            pltpu.make_async_copy(cells_h, cells_v, local_sem.at[3]),
            pltpu.make_async_copy(seeds_h, seeds_s, local_sem.at[4]),
            pltpu.make_async_copy(count_h, count_s, local_sem.at[5]),
            pltpu.make_async_copy(weight_h, weight_v, local_sem.at[6]),
        ]
        for load in loads:
            load.start()
        for load in loads[:3]:
            load.wait()
        pl.semaphore_wait(barrier, len(peers))

        sends = []
        for n, (dx, dy) in enumerate(near):
            copy = pltpu.make_async_remote_copy(
                src_ref=coef.at[:, edge_r[dx], edge_c[dy]],
                dst_ref=coef.at[:, halo_r[-dx], halo_c[-dy]],
                send_sem=coef_send.at[n], recv_sem=coef_recv.at[n],
                device_id=at(dx, dy), device_id_type=MESH)
            copy.start()
            sends.append(copy)
        coef_copies = list(sends)

        for load in loads[3:6]:
            load.wait()
        slots = cells_v.shape[1]
        cell = cells_v[...]
        sensor_r = lax.div(cell, cols)
        sensor_c = lax.rem(cell, cols)
        sub = iota((8, slots), 0)
        seed = jnp.where(sub == 0, seeds_s[0, 0], 0)
        for k in range(1, probes):
            seed = jnp.where(sub == k, seeds_s[0, k], seed)
        live = iota((8, slots), 1) < count_s[0, 0]
        keep = jnp.logical_and(live, sub < probes)
        sampled = mix(seed * 668265261 + position(gx * rows + sensor_r, gy * cols + sensor_c))
        sampled = jnp.where(keep, sampled, 0.0)
        loads[6].wait()
        weight = weight_v[...]
        weighted = jnp.dot(sampled, weight, precision=lax.Precision.HIGHEST, preferred_element_type=F32)
        weighted = jnp.where(keep, weighted, 0.0)
        row_f, col_f = sensor_r.astype(F32), sensor_c.astype(F32)
        message = jnp.where(sub == probes, jnp.broadcast_to(row_f, (8, slots)), weighted)
        message = jnp.where(sub == probes + 1, jnp.broadcast_to(col_f, (8, slots)), message)
        w_send[...] = message
        obs_copies = []
        for n, (dx, dy) in enumerate(cross):
            copy = pltpu.make_async_remote_copy(
                src_ref=w_send, dst_ref=w_recv.at[n],
                send_sem=obs_send.at[n], recv_sem=obs_recv.at[n],
                device_id=at(dx, dy), device_id_type=MESH)
            copy.start()
            obs_copies.append(copy)
            sends.append(copy)

        row_ids = (gx * rows - PAD_R + iota((ext_r, ext_c), 0)) & (nx - 1)
        col_ids = (gy * cols - PAD_C + iota((ext_r, ext_c), 1)) & (ny - 1)
        place = position(row_ids, col_ids)
        for k in range(probes):
            prob[k] = mix(seeds_s[0, k] * 668265261 + place)

        in_row = (iota((rows, slots), 0) == sensor_r).astype(F32)
        in_col = (iota((cols, slots), 0) == sensor_c).astype(F32).astype(BF16)
        spread = jnp.concatenate([in_row * weighted[k:k + 1] for k in range(probes)], axis=0)
        own = times(spread, in_col, NT)

        for copy in coef_copies:
            copy.wait_recv()
        damp, cx, cy = coef[0], coef[1], coef[2]
        cxu, cyl = pltpu.roll(cx, 1, 0), pltpu.roll(cy, 1, 1)
        up_v[...] = cxu
        left_v[...] = cyl
        diag_v[...] = damp + cx + cxu + cy + cyl

        def operator(field):
            return (diag_v[...] * field - coef[1] * pltpu.roll(field, ext_r - 1, 0) - up_v[...] * pltpu.roll(field, 1, 0)
                    - coef[2] * pltpu.roll(field, ext_c - 1, 1) - left_v[...] * pltpu.roll(field, 1, 1))

        for k in range(probes):
            once[k] = operator(prob[k])
        for k in range(probes):
            image[k] = operator(once[k])
            image[k, r_in, c_in] = image[k, r_in, c_in] + own[k * rows:(k + 1) * rows]

        for copy in obs_copies:
            copy.wait_recv()

        def side(n, column, lane):
            text = w_recv[n]
            r, c = text[probes:probes + 1], text[probes + 1:probes + 2]
            hit = jnp.logical_and(c == float(column), iota((PAD_C, slots), 0) == lane)
            in_r = (iota((rows, slots), 0).astype(F32) == r).astype(F32)
            lhs = jnp.concatenate([in_r * text[k:k + 1] for k in range(probes)], axis=0)
            return times(lhs, hit.astype(F32).astype(BF16), NT)

        def end(n, row):
            text = w_recv[n]
            r, c = text[probes:probes + 1], text[probes + 1:probes + 2]
            in_c = (iota((cols, slots), 0).astype(F32) == c).astype(F32).astype(BF16)
            return times(jnp.where(r == float(row), text, 0.0), in_c, NT)

        from_left = side(0, cols - 1, PAD_C - 1)
        from_right = side(1, 0, 0)
        from_above = end(2, rows - 1)
        from_below = end(3, 0)
        for k in range(probes):
            mine = slice(k * rows, (k + 1) * rows)
            image[k, r_in, halo_c[-1]] = image[k, r_in, halo_c[-1]] + from_left[mine]
            image[k, r_in, halo_c[1]] = image[k, r_in, halo_c[1]] + from_right[mine]
            image[k, PAD_R - 1:PAD_R, c_in] = image[k, PAD_R - 1:PAD_R, c_in] + from_above[k:k + 1]
            image[k, PAD_R + rows:PAD_R + rows + 1, c_in] = (
                image[k, PAD_R + rows:PAD_R + rows + 1, c_in] + from_below[k:k + 1])

        def fold(x):
            total = jnp.sum(x.reshape(rows // 8, 8, cols), axis=0)
            total = sum(total[:, n * 128:(n + 1) * 128] for n in range(cols // 128))
            return jnp.sum(total, axis=0, keepdims=True)

        block = jnp.concatenate([image[k, r_in, c_in] for k in range(probes)], axis=0)
        picked = times(block, in_col)
        seen = [jnp.sum(picked[k * rows:(k + 1) * rows] * in_row, axis=0, keepdims=True) for k in range(probes)]
        seen = jnp.concatenate(seen + [jnp.zeros((8 - probes, slots), F32)], axis=0)
        seen = jnp.where(keep, seen, 0.0)
        answer = jnp.dot(seen, weight, precision=lax.Precision.HIGHEST, preferred_element_type=F32)
        quad = seen * answer
        quad = sum(quad[:, n * 128:(n + 1) * 128] for n in range(slots // 128))
        firsts, seconds, thirds = [], [], []
        for k in range(probes):
            field = image[k]
            inner = field[r_in, c_in]
            firsts.append(fold(prob[k, r_in, c_in] * inner))
            seconds.append(fold(inner * inner))
            twice = operator(field)[r_in, c_in]
            thirds.append(fold(twice * twice) + quad[k:k + 1])
        lines = jnp.concatenate(firsts + seconds + thirds + [jnp.zeros((16 - 3 * probes, 128), F32)], axis=0)
        sums = jnp.sum(lines, axis=1, keepdims=True)
        total = jnp.sum(jnp.where(iota((16, 128), 0) == iota((16, 128), 1), sums, 0.0), axis=0, keepdims=True)

        for stage, (size, got, ssem, rsem) in enumerate(((by, got_y, y_send, y_recv), (bx, got_x, x_send, x_recv))):
            part[stage] = total
            copies = []
            for d in range(1, size):
                copy = pltpu.make_async_remote_copy(
                    src_ref=part.at[stage], dst_ref=got.at[d - 1],
                    send_sem=ssem.at[d - 1], recv_sem=rsem.at[d - 1],
                    device_id=at(0, d) if stage == 0 else at(d, 0), device_id_type=MESH)
                copy.start()
                copies.append(copy)
            for d, copy in enumerate(copies):
                copy.wait_recv()
                total = total + got[d]
            sends += copies

        lane = iota((1, 128), 1)
        m1 = jnp.where(lane < probes, total, 1.0)
        m2 = jnp.where(lane < probes, pltpu.roll(total, 128 - probes, 1), 1.0)
        m3 = jnp.where(lane < probes, pltpu.roll(total, 128 - 2 * probes, 1), 1.0)
        norm0 = float(nx * ny)
        alpha0 = norm0 / m1
        norm1 = alpha0 * alpha0 * m2 - norm0
        alpha1 = norm1 / (alpha0 * alpha0 * (m3 - m2 * m2 / m1))
        on_probe = alpha0 + alpha1 * (1.0 + norm1 / norm0)
        on_image = alpha1 * alpha0
        trace = jnp.sum(jnp.where(lane < probes, alpha0 * norm0 + alpha1 * norm1, 0.0)) / probes
        trace_ref[0, 0] = trace
        for k in range(probes):
            sol_ref[k] = on_probe[0, k] * prob[k, r_in, c_in] - on_image[0, k] * image[k, r_in, c_in]
        for copy in sends:
            copy.wait_send()

    return body, ext_r, ext_c


def solution(mesh):
    bx, by = mesh.shape["gx"], mesh.shape["gy"]

    def per_device(probe_seeds, damping, coupling_x, coupling_y, sensor_count, sensor_cells, obs_weight):
        probes = probe_seeds.shape[0]
        rows, cols = damping.shape
        slots = sensor_cells.shape[-1]
        body, ext_r, ext_c = kernel_of(probes, bx, by, rows, cols)
        dma = pltpu.SemaphoreType.DMA
        sol, trace = pl.pallas_call(
            body,
            name="two_steps",
            out_shape=(jax.ShapeDtypeStruct((probes, rows, cols), F32), jax.ShapeDtypeStruct((1, 1), F32)),
            in_specs=[pl.BlockSpec(memory_space=pl.ANY)] * 7,
            out_specs=(pl.BlockSpec(memory_space=pltpu.VMEM), pl.BlockSpec(memory_space=pltpu.SMEM)),
            scratch_shapes=[
                pltpu.SMEM((1, probes), jnp.int32), pltpu.SMEM((1, 1), jnp.int32),
                pltpu.VMEM((1, slots), jnp.int32), pltpu.VMEM((slots, slots), F32),
                pltpu.VMEM((3, ext_r, ext_c), F32),
                pltpu.VMEM((ext_r, ext_c), F32), pltpu.VMEM((ext_r, ext_c), F32), pltpu.VMEM((ext_r, ext_c), F32),
                pltpu.VMEM((probes, ext_r, ext_c), F32), pltpu.VMEM((probes, ext_r, ext_c), F32),
                pltpu.VMEM((probes, ext_r, ext_c), F32),
                pltpu.VMEM((8, slots), F32), pltpu.VMEM((4, 8, slots), F32),
                pltpu.VMEM((2, 1, 128), F32), pltpu.VMEM((by - 1, 1, 128), F32), pltpu.VMEM((bx - 1, 1, 128), F32),
                dma((7,)), dma((8,)), dma((8,)), dma((4,)), dma((4,)),
                dma((by - 1,)), dma((by - 1,)), dma((bx - 1,)), dma((bx - 1,)),
            ],
            compiler_params=pltpu.CompilerParams(collective_id=0, has_side_effects=True),
        )(probe_seeds.reshape(1, probes), damping, coupling_x, coupling_y, sensor_count,
          sensor_cells.reshape(1, slots), obs_weight.reshape(slots, slots))
        return sol, trace.reshape(())

    return jax.shard_map(
        per_device,
        mesh=mesh,
        in_specs=(P(), P("gx", "gy"), P("gx", "gy"), P("gx", "gy"), P("gx", "gy"),
                  P("gx", "gy", None), P("gx", "gy", None, None)),
        out_specs=(P(None, "gx", "gy"), P()),
        check_vma=False,
    )
```

```python
import jax
import jax.numpy as jnp
from jax import lax
from jax.experimental import pallas as pl
from jax.experimental.pallas import tpu as pltpu
from jax.sharding import PartitionSpec as P

MESH = pl.DeviceIdType.MESH
NT = (((1,), (1,)), ((), ()))
F32 = jnp.float32
BF16 = jnp.bfloat16

PAD_R, PAD_C = 8, 128
GROUP = 16


def mix(base):
    mixed = (base ^ ((base >> 16) & 65535)) * 73244475
    mixed = (mixed ^ ((mixed >> 16) & 65535)) * 73244475
    mixed = mixed ^ ((mixed >> 16) & 65535)
    return (2 * ((mixed >> 7) & 1) - 1).astype(F32)


def position(rows, cols):
    return rows * 374761393 + cols * 1103515245


def iota(shape, dim):
    return lax.broadcasted_iota(jnp.int32, shape, dim)


def split3(x):
    high = x.astype(BF16)
    rest = x - high.astype(F32)
    mid = rest.astype(BF16)
    low = (rest - mid.astype(F32)).astype(BF16)
    return high, mid, low


def times(x, y, dims=(((1,), (0,)), ((), ()))):
    total = None
    for part in reversed(split3(x)):
        one = lax.dot_general(part, y, dims, preferred_element_type=F32)
        total = one if total is None else total + one
    return total


def hbm(x):
    return pltpu.with_memory_space_constraint(x, pltpu.HBM)


def kernel_of(probes, bx, by, rows, cols):
    ext_r, ext_c = rows + PAD_R, cols + PAD_C
    nx, ny = bx * rows, by * cols
    r_in, c_in = slice(0, rows), slice(0, cols)
    r_out, c_out = slice(rows, ext_r), slice(cols, ext_c)
    tiles = rows // 8
    cross = [(0, 1), (0, -1), (1, 0), (-1, 0)]
    corners = [(a, b) for a in (-1, 1) for b in (-1, 1)]

    def body(seeds_h, damp_h, cx_h, cy_h, count_s, cells_h, weight_h, image_h, prob_h, total_ref,
             seeds_s, cells_v, weight_v, coef, up_v, left_v, diag_v, prob, once, image, inner_v,
             edge_v, col_send, row_recv, col_recv, diag_recv, w_send, w_recv, part, got_y, got_x,
             local_sem, coef_send, coef_recv, obs_send, obs_recv, y_send, y_recv, x_send, x_recv):
        gx, gy = lax.axis_index("gx"), lax.axis_index("gy")

        def at(dx, dy):
            return (lax.rem(gx + (dx + bx), bx), lax.rem(gy + (dy + by), by))

        barrier = pltpu.get_barrier_semaphore()
        nearest = [(0, 1), (0, by - 1), (1, 0), (bx - 1, 0)] + corners
        peers = nearest + [(0, d) for d in range(2, by - 1)] + [(d, 0) for d in range(2, bx - 1)]
        for dx, dy in peers:
            pl.semaphore_signal(barrier, inc=1, device_id=at(dx, dy), device_id_type=MESH)

        loads = [
            pltpu.make_async_copy(damp_h, coef.at[0, r_in, c_in], local_sem.at[0]),
            pltpu.make_async_copy(cx_h, coef.at[1, r_in, c_in], local_sem.at[1]),
            pltpu.make_async_copy(cy_h, coef.at[2, r_in, c_in], local_sem.at[2]),
            pltpu.make_async_copy(cells_h, cells_v, local_sem.at[3]),
            pltpu.make_async_copy(seeds_h, seeds_s, local_sem.at[4]),
            pltpu.make_async_copy(weight_h, weight_v, local_sem.at[5]),
        ]
        for load in loads:
            load.start()
        for load in loads[:3]:
            load.wait()

        lane = iota((rows, 128), 1)
        for n, (start, base) in enumerate(((cols - 128, 3), (0, 0))):
            d, x, y = (coef[i, r_in, start:start + 128] for i in range(3))
            d = pltpu.roll(d, base, 1) if base else d
            edge = jnp.where(lane < 3, d, jnp.where(lane < 6, pltpu.roll(x, base + 3, 1), pltpu.roll(y, base + 6, 1)))
            edge_v[n] = edge
            tile = edge[0:8]
            for a in range(1, tiles):
                tile = jnp.where(lane[0:8] < a * GROUP, tile, pltpu.roll(edge[8 * a:8 * a + 8], a * GROUP, 1))
            col_send[n] = tile
        pl.semaphore_wait(barrier, len(peers))

        sends = []

        def send(src, dst, ssem, rsem, dx, dy):
            copy = pltpu.make_async_remote_copy(
                src_ref=src, dst_ref=dst, send_sem=ssem, recv_sem=rsem,
                device_id=at(dx, dy), device_id_type=MESH)
            copy.start()
            sends.append(copy)
            return copy

        coef_copies = [
            send(col_send.at[n], col_recv.at[n], coef_send.at[n], coef_recv.at[n], 0, 1 - 2 * n) for n in range(2)
        ] + [
            send(coef.at[:, rows - 8:rows, c_in] if n == 0 else coef.at[:, 0:8, c_in], row_recv.at[n],
                 coef_send.at[2 + n], coef_recv.at[2 + n], 1 - 2 * n, 0) for n in range(2)
        ] + [
            send(edge_v.at[m, rows - 8:rows] if n == 0 else edge_v.at[m, 0:8], diag_recv.at[n, m],
                 coef_send.at[4 + 2 * n + m], coef_recv.at[4 + 2 * n + m], 1 - 2 * n, 1 - 2 * m)
            for n in range(2) for m in range(2)
        ]

        for load in loads[3:5]:
            load.wait()
        slots = cells_v.shape[1]
        cell = cells_v[...]
        sensor_r = lax.div(cell, cols)
        sensor_c = lax.rem(cell, cols)
        sub = iota((8, slots), 0)
        seed = jnp.where(sub == 0, seeds_s[0, 0], 0)
        for k in range(1, probes):
            seed = jnp.where(sub == k, seeds_s[0, k], seed)
        live = iota((8, slots), 1) < count_s[0, 0]
        keep = jnp.logical_and(live, sub < probes)
        sampled = mix(seed * 668265261 + position(gx * rows + sensor_r, gy * cols + sensor_c))
        sampled = jnp.where(keep, sampled, 0.0)
        loads[5].wait()
        weight = weight_v[...]
        weighted = jnp.dot(sampled, weight, precision=lax.Precision.HIGHEST, preferred_element_type=F32)
        weighted = jnp.where(keep, weighted, 0.0)
        row_f, col_f = sensor_r.astype(F32), sensor_c.astype(F32)
        message = jnp.where(sub == probes, jnp.broadcast_to(row_f, (8, slots)), weighted)
        message = jnp.where(sub == probes + 1, jnp.broadcast_to(col_f, (8, slots)), message)
        w_send[...] = message
        obs_copies = [
            send(w_send, w_recv.at[n], obs_send.at[n], obs_recv.at[n], dx, dy) for n, (dx, dy) in enumerate(cross)
        ]

        row_ids, col_ids = iota((ext_r, ext_c), 0), iota((ext_r, ext_c), 1)
        row_ids = jnp.where(row_ids < rows + PAD_R // 2, row_ids, row_ids - ext_r)
        col_ids = jnp.where(col_ids < cols + PAD_C // 2, col_ids, col_ids - ext_c)
        place = position((gx * rows + row_ids) & (nx - 1), (gy * cols + col_ids) & (ny - 1))
        for k in range(probes):
            prob[k] = mix(seeds_s[0, k] * 668265261 + place)
        saves = [pltpu.make_async_copy(prob.at[:, r_in, c_in], prob_h, local_sem.at[6])]
        saves[0].start()

        in_row = (iota((rows, slots), 0) == sensor_r).astype(F32)
        in_col = (iota((cols, slots), 0) == sensor_c).astype(F32).astype(BF16)
        spread = jnp.concatenate([in_row * weighted[k:k + 1] for k in range(probes)], axis=0)
        own = times(spread, in_col, NT)

        for copy in coef_copies:
            copy.wait_recv()
        right = lane[0:8] < 64
        below = iota((8, 128), 0) < 4
        from_left, from_right = col_recv[0], col_recv[1]
        for i in range(3):
            for a in range(tiles):
                coef[i, 8 * a:8 * a + 8, c_out] = jnp.where(
                    right, pltpu.roll(from_right, (256 - 3 * i - a * GROUP) % 128, 1),
                    pltpu.roll(from_left, (256 + 125 - 3 * i - a * GROUP) % 128, 1))
            coef[i, r_out, c_in] = jnp.where(iota((8, cols), 0) < 4, row_recv[1, i], row_recv[0, i])
            corner = [[pltpu.roll(diag_recv[n, m], (256 + 125 * (1 - m) - 3 * i) % 128, 1) for m in range(2)]
                      for n in range(2)]
            coef[i, r_out, c_out] = jnp.where(
                below, jnp.where(right, corner[1][1], corner[1][0]), jnp.where(right, corner[0][1], corner[0][0]))
        damp, cx, cy = coef[0], coef[1], coef[2]
        cxu, cyl = pltpu.roll(cx, 1, 0), pltpu.roll(cy, 1, 1)
        up_v[...] = cxu
        left_v[...] = cyl
        diag_v[...] = damp + cx + cxu + cy + cyl

        def operator(field):
            return (diag_v[...] * field - coef[1] * pltpu.roll(field, ext_r - 1, 0) - up_v[...] * pltpu.roll(field, 1, 0)
                    - coef[2] * pltpu.roll(field, ext_c - 1, 1) - left_v[...] * pltpu.roll(field, 1, 1))

        for k in range(probes):
            once[k] = operator(prob[k])

        for copy in obs_copies:
            copy.wait_recv()

        def side(n, column, at_lane):
            text = w_recv[n]
            r, c = text[probes:probes + 1], text[probes + 1:probes + 2]
            hit = jnp.logical_and(c == float(column), iota((PAD_C, slots), 0) == at_lane)
            in_r = (iota((rows, slots), 0).astype(F32) == r).astype(F32)
            lhs = jnp.concatenate([in_r * text[k:k + 1] for k in range(probes)], axis=0)
            return times(lhs, hit.astype(F32).astype(BF16), NT)

        def end(n, row):
            text = w_recv[n]
            r, c = text[probes:probes + 1], text[probes + 1:probes + 2]
            in_c = (iota((cols, slots), 0).astype(F32) == c).astype(F32).astype(BF16)
            return times(jnp.where(r == float(row), text, 0.0), in_c, NT)

        beside = side(0, cols - 1, PAD_C - 1) + side(1, 0, 0)
        above_obs = end(2, rows - 1)
        below_obs = end(3, 0)
        for k in range(probes):
            mine = slice(k * rows, (k + 1) * rows)
            image[k] = operator(once[k])
            inner = image[k, r_in, c_in] + own[mine]
            image[k, r_in, c_in] = inner
            inner_v[k] = inner
            image[k, r_in, c_out] = image[k, r_in, c_out] + beside[mine]
            image[k, ext_r - 1:ext_r, c_in] = image[k, ext_r - 1:ext_r, c_in] + above_obs[k:k + 1]
            image[k, rows:rows + 1, c_in] = image[k, rows:rows + 1, c_in] + below_obs[k:k + 1]
        saves.append(pltpu.make_async_copy(inner_v, image_h, local_sem.at[7]))
        saves[1].start()

        def fold(x):
            total = jnp.sum(x.reshape(rows // 8, 8, cols), axis=0)
            total = sum(total[:, n * 128:(n + 1) * 128] for n in range(cols // 128))
            return jnp.sum(total, axis=0, keepdims=True)

        block = jnp.concatenate([image[k, r_in, c_in] for k in range(probes)], axis=0)
        picked = times(block, in_col)
        seen = [jnp.sum(picked[k * rows:(k + 1) * rows] * in_row, axis=0, keepdims=True) for k in range(probes)]
        seen = jnp.concatenate(seen + [jnp.zeros((8 - probes, slots), F32)], axis=0)
        seen = jnp.where(keep, seen, 0.0)
        answer = jnp.dot(seen, weight, precision=lax.Precision.HIGHEST, preferred_element_type=F32)
        quad = seen * answer
        quad = sum(quad[:, n * 128:(n + 1) * 128] for n in range(slots // 128))
        firsts, seconds, thirds = [], [], []
        for k in range(probes):
            field = image[k]
            inner = field[r_in, c_in]
            firsts.append(fold(prob[k, r_in, c_in] * inner))
            seconds.append(fold(inner * inner))
            twice = operator(field)[r_in, c_in]
            thirds.append(fold(twice * twice) + quad[k:k + 1])
        lines = jnp.concatenate(firsts + seconds + thirds + [jnp.zeros((16 - 3 * probes, 128), F32)], axis=0)
        sums = jnp.sum(lines, axis=1, keepdims=True)
        total = jnp.sum(jnp.where(iota((16, 128), 0) == iota((16, 128), 1), sums, 0.0), axis=0, keepdims=True)

        for stage, (size, got, ssem, rsem) in enumerate(((by, got_y, y_send, y_recv), (bx, got_x, x_send, x_recv))):
            part[stage] = total
            copies = [
                send(part.at[stage], got.at[d - 1], ssem.at[d - 1], rsem.at[d - 1], *((0, d) if stage == 0 else (d, 0)))
                for d in range(1, size)
            ]
            for d, copy in enumerate(copies):
                copy.wait_recv()
                total = total + got[d]
        total_ref[...] = total
        for save in saves:
            save.wait()
        for copy in sends:
            copy.wait_send()

    def finish(total_ref, image_ref, prob_ref, sol_ref, trace_ref):
        total = total_ref[...]
        lane = iota((1, 128), 1)
        m1 = jnp.where(lane < probes, total, 1.0)
        m2 = jnp.where(lane < probes, pltpu.roll(total, 128 - probes, 1), 1.0)
        m3 = jnp.where(lane < probes, pltpu.roll(total, 128 - 2 * probes, 1), 1.0)
        norm0 = float(nx * ny)
        alpha0 = norm0 / m1
        norm1 = alpha0 * alpha0 * m2 - norm0
        alpha1 = norm1 / (alpha0 * alpha0 * (m3 - m2 * m2 / m1))
        on_probe = alpha0 + alpha1 * (1.0 + norm1 / norm0)
        on_image = alpha1 * alpha0
        trace_ref[0, 0] = jnp.sum(jnp.where(lane < probes, alpha0 * norm0 + alpha1 * norm1, 0.0)) / probes
        for k in range(probes):
            sol_ref[k] = on_probe[0, k] * prob_ref[k] - on_image[0, k] * image_ref[k]

    return body, finish, ext_r, ext_c


def solution(mesh):
    bx, by = mesh.shape["gx"], mesh.shape["gy"]

    def per_device(probe_seeds, damping, coupling_x, coupling_y, sensor_count, sensor_cells, obs_weight):
        probes = probe_seeds.shape[0]
        rows, cols = damping.shape
        slots = sensor_cells.shape[-1]
        body, finish, ext_r, ext_c = kernel_of(probes, bx, by, rows, cols)
        dma = pltpu.SemaphoreType.DMA
        plane = pltpu.VMEM((ext_r, ext_c), F32)
        fields = pltpu.VMEM((probes, ext_r, ext_c), F32)
        in_vmem = pl.BlockSpec(memory_space=pltpu.VMEM)
        in_hbm = pl.BlockSpec(memory_space=pltpu.HBM)
        in_smem = pl.BlockSpec(memory_space=pltpu.SMEM)
        field = jax.ShapeDtypeStruct((probes, rows, cols), F32)
        image, prob, total = pl.pallas_call(
            body,
            name="two_steps",
            out_shape=(field, field, jax.ShapeDtypeStruct((1, 128), F32)),
            in_specs=[in_hbm] * 4 + [in_smem] + [in_hbm] * 2,
            out_specs=(pl.BlockSpec(memory_space=pl.ANY), pl.BlockSpec(memory_space=pl.ANY), in_vmem),
            scratch_shapes=[
                pltpu.SMEM((1, probes), jnp.int32),
                pltpu.VMEM((1, slots), jnp.int32), pltpu.VMEM((slots, slots), F32),
                pltpu.VMEM((3, ext_r, ext_c), F32), plane, plane, plane, fields, fields, fields,
                pltpu.VMEM((probes, rows, cols), F32),
                pltpu.VMEM((2, rows, 128), F32), pltpu.VMEM((2, 8, 128), F32),
                pltpu.VMEM((2, 3, 8, cols), F32), pltpu.VMEM((2, 8, 128), F32), pltpu.VMEM((2, 2, 8, 128), F32),
                pltpu.VMEM((8, slots), F32), pltpu.VMEM((4, 8, slots), F32),
                pltpu.VMEM((2, 1, 128), F32), pltpu.VMEM((by - 1, 1, 128), F32), pltpu.VMEM((bx - 1, 1, 128), F32),
                dma((8,)), dma((8,)), dma((8,)), dma((4,)), dma((4,)),
                dma((by - 1,)), dma((by - 1,)), dma((bx - 1,)), dma((bx - 1,)),
            ],
            compiler_params=pltpu.CompilerParams(
                collective_id=0, has_side_effects=True, vmem_limit_bytes=16 * 2**20),
        )(hbm(probe_seeds.reshape(1, probes)), hbm(damping), hbm(coupling_x), hbm(coupling_y), sensor_count,
          hbm(sensor_cells.reshape(1, slots)), hbm(obs_weight.reshape(slots, slots)))
        sol, trace = pl.pallas_call(
            finish,
            name="finish",
            out_shape=(field, jax.ShapeDtypeStruct((1, 1), F32)),
            in_specs=[in_vmem] * 3,
            out_specs=(in_vmem, in_smem),
            compiler_params=pltpu.CompilerParams(vmem_limit_bytes=16 * 2**20),
        )(total, image, prob)
        return sol, trace.reshape(())

    return jax.shard_map(
        per_device,
        mesh=mesh,
        in_specs=(P(), P("gx", "gy"), P("gx", "gy"), P("gx", "gy"), P("gx", "gy"),
                  P("gx", "gy", None), P("gx", "gy", None, None)),
        out_specs=(P(None, "gx", "gy"), P()),
        check_vma=False,
    )
```

```python
import jax
import jax.numpy as jnp
from jax import lax
from jax.experimental import pallas as pl
from jax.experimental.pallas import tpu as pltpu
from jax.sharding import PartitionSpec as P

MESH = pl.DeviceIdType.MESH
NT = (((1,), (1,)), ((), ()))
F32 = jnp.float32
BF16 = jnp.bfloat16

PAD_R, PAD_C = 8, 128
GROUP = 16


def mix(base):
    mixed = (base ^ ((base >> 16) & 65535)) * 73244475
    mixed = (mixed ^ ((mixed >> 16) & 65535)) * 73244475
    mixed = mixed ^ ((mixed >> 16) & 65535)
    return (2 * ((mixed >> 7) & 1) - 1).astype(F32)


def position(rows, cols):
    return rows * 374761393 + cols * 1103515245


def iota(shape, dim):
    return lax.broadcasted_iota(jnp.int32, shape, dim)


def split3(x):
    high = x.astype(BF16)
    rest = x - high.astype(F32)
    mid = rest.astype(BF16)
    low = (rest - mid.astype(F32)).astype(BF16)
    return high, mid, low


def times(x, y, dims=(((1,), (0,)), ((), ()))):
    total = None
    for part in reversed(split3(x)):
        one = lax.dot_general(part, y, dims, preferred_element_type=F32)
        total = one if total is None else total + one
    return total


def hbm(x):
    return pltpu.with_memory_space_constraint(x, pltpu.HBM)


def kernel_of(probes, bx, by, rows, cols):
    ext_r, ext_c = rows + PAD_R, cols + PAD_C
    nx, ny = bx * rows, by * cols
    r_in, c_in = slice(0, rows), slice(0, cols)
    r_out, c_out = slice(rows, ext_r), slice(cols, ext_c)
    tiles = rows // 8
    cross = [(0, 1), (0, -1), (1, 0), (-1, 0)]
    corners = [(a, b) for a in (-1, 1) for b in (-1, 1)]

    def body(seeds_h, damp_h, cx_h, cy_h, count_s, cells_h, weight_h, image_h, prob_h, total_ref,
             seeds_s, cells_v, weight_v, coef, up_v, left_v, diag_v, prob, once, image, inner_v,
             edge_v, col_send, row_send, row_recv, col_recv, diag_recv, w_send, w_recv, part, got_y, got_x,
             local_sem, known_sem, coef_send, coef_recv, obs_send, obs_recv, y_send, y_recv, x_send, x_recv):
        gx, gy = lax.axis_index("gx"), lax.axis_index("gy")

        def at(dx, dy):
            return (lax.rem(gx + (dx + bx), bx), lax.rem(gy + (dy + by), by))

        barrier = pltpu.get_barrier_semaphore()
        nearest = [(0, 1), (0, by - 1), (1, 0), (bx - 1, 0)] + corners
        for dx, dy in nearest:
            pl.semaphore_signal(barrier, inc=1, device_id=at(dx, dy), device_id_type=MESH)

        loads = [
            pltpu.make_async_copy(damp_h, coef.at[0, r_in, c_in], local_sem.at[0]),
            pltpu.make_async_copy(cx_h, coef.at[1, r_in, c_in], local_sem.at[1]),
            pltpu.make_async_copy(cy_h, coef.at[2, r_in, c_in], local_sem.at[2]),
            pltpu.make_async_copy(cells_h, cells_v, local_sem.at[3]),
            pltpu.make_async_copy(seeds_h, seeds_s, local_sem.at[4]),
            pltpu.make_async_copy(weight_h, weight_v, local_sem.at[5]),
        ]
        for load in loads:
            load.start()
        for load in loads[:3]:
            load.wait()

        lane = iota((rows, 128), 1)
        for n, (start, base) in enumerate(((cols - 128, 3), (0, 0))):
            d, x, y = (coef[i, r_in, start:start + 128] for i in range(3))
            d = pltpu.roll(d, base, 1) if base else d
            edge = jnp.where(lane < 3, d, jnp.where(lane < 6, pltpu.roll(x, base + 3, 1), pltpu.roll(y, base + 6, 1)))
            edge_v[n] = edge
            tile = edge[0:8]
            for a in range(1, tiles):
                tile = jnp.where(lane[0:8] < a * GROUP, tile, pltpu.roll(edge[8 * a:8 * a + 8], a * GROUP, 1))
            col_send[n] = tile
        for n, base in enumerate((rows - 3, 0)):
            row_send[n, 0:2] = coef[0, base + 1 - n:base + 3 - n, c_in]
            row_send[n, 2:5] = coef[1, base:base + 3, c_in]
            row_send[n, 5:7] = coef[2, base + 1 - n:base + 3 - n, c_in]
            row_send[n, 7:8] = coef[2, base:base + 1, c_in]
        for load in loads[3:5]:
            load.wait()
        slots = cells_v.shape[1]
        cell = cells_v[...]
        sensor_r = lax.div(cell, cols)
        sensor_c = lax.rem(cell, cols)
        sub = iota((8, slots), 0)
        seed = jnp.where(sub == 0, seeds_s[0, 0], 0)
        for k in range(1, probes):
            seed = jnp.where(sub == k, seeds_s[0, k], seed)
        live = iota((8, slots), 1) < count_s[0, 0]
        keep = jnp.logical_and(live, sub < probes)
        sampled = mix(seed * 668265261 + position(gx * rows + sensor_r, gy * cols + sensor_c))
        sampled = jnp.where(keep, sampled, 0.0)
        loads[5].wait()
        weight = split3(weight_v[...])

        def weigh(x):
            high, mid, low = split3(x)
            parts = (jnp.concatenate([high, mid, low], axis=0), jnp.concatenate([high, mid], axis=0), high)
            done = [jnp.dot(x_part, w_part, preferred_element_type=F32) for x_part, w_part in zip(parts, weight)]
            return ((done[0][16:24] + done[1][8:16] + done[2]) + (done[0][8:16] + done[1][0:8])) + done[0][0:8]

        exact = sampled.astype(BF16)
        weighted = sum(jnp.dot(exact, part, preferred_element_type=F32) for part in reversed(weight))
        weighted = jnp.where(keep, weighted, 0.0)
        row_f, col_f = sensor_r.astype(F32), sensor_c.astype(F32)
        message = jnp.where(sub == probes, jnp.broadcast_to(row_f, (8, slots)), weighted)
        message = jnp.where(sub == probes + 1, jnp.broadcast_to(col_f, (8, slots)), message)
        w_send[...] = message

        pl.semaphore_wait(barrier, len(nearest))

        assert (bx, by) == (32, 16)

        def hail(axis, step):
            for m, d in enumerate((2**step, -2**step)):
                pl.semaphore_signal(known_sem.at[axis, step, m], inc=1, device_id=at(*((d, 0), (0, d))[axis]),
                                    device_id_type=MESH)

        def heard(axis, step):
            for m in range(2):
                pl.semaphore_wait(known_sem.at[axis, step, m], 1)

        def relay(axis, step):
            heard(axis, step)
            hail(axis, step + 1)

        hail(0, 0)
        hail(1, 0)

        sends = []

        def send(src, dst, ssem, rsem, dx, dy):
            copy = pltpu.make_async_remote_copy(
                src_ref=src, dst_ref=dst, send_sem=ssem, recv_sem=rsem,
                device_id=at(dx, dy), device_id_type=MESH)
            copy.start()
            sends.append(copy)
            return copy

        coef_copies = [
            send(edge_v.at[m, rows - 8:rows] if n == 0 else edge_v.at[m, 0:8], diag_recv.at[n, m],
                 coef_send.at[4 + 2 * n + m], coef_recv.at[4 + 2 * n + m], 1 - 2 * n, 1 - 2 * m)
            for n in range(2) for m in range(2)
        ] + [
            send(row_send.at[n], row_recv.at[n], coef_send.at[2 + n], coef_recv.at[2 + n], 1 - 2 * n, 0)
            for n in range(2)
        ] + [
            send(col_send.at[n], col_recv.at[n], coef_send.at[n], coef_recv.at[n], 0, 1 - 2 * n) for n in range(2)
        ]

        obs_copies = [
            send(w_send, w_recv.at[n], obs_send.at[n], obs_recv.at[n], dx, dy) for n, (dx, dy) in enumerate(cross)
        ]

        row_ids, col_ids = iota((ext_r, ext_c), 0), iota((ext_r, ext_c), 1)
        row_ids = jnp.where(row_ids < rows + PAD_R // 2, row_ids, row_ids - ext_r)
        col_ids = jnp.where(col_ids < cols + PAD_C // 2, col_ids, col_ids - ext_c)
        place = position((gx * rows + row_ids) & (nx - 1), (gy * cols + col_ids) & (ny - 1))
        for k in range(probes):
            prob[k] = mix(seeds_s[0, k] * 668265261 + place)
        saves = [pltpu.make_async_copy(prob.at[:, r_in, c_in], prob_h, local_sem.at[6])]
        saves[0].start()

        in_row = (iota((rows, slots), 0) == sensor_r).astype(F32)
        in_col = (iota((cols, slots), 0) == sensor_c).astype(F32).astype(BF16)
        spread = jnp.concatenate([in_row * weighted[k:k + 1] for k in range(probes)], axis=0)
        own = times(spread, in_col, NT)

        relay(1, 0)
        relay(0, 0)

        for copy in obs_copies:
            copy.wait_recv()

        def side(n, column, at_lane):
            text = w_recv[n]
            r, c = text[probes:probes + 1], text[probes + 1:probes + 2]
            hit = jnp.logical_and(c == float(column), iota((PAD_C, slots), 0) == at_lane)
            in_r = (iota((rows, slots), 0).astype(F32) == r).astype(F32)
            lhs = jnp.concatenate([in_r * text[k:k + 1] for k in range(probes)], axis=0)
            return times(lhs, hit.astype(F32).astype(BF16), NT)

        def end(n, row):
            text = w_recv[n]
            r, c = text[probes:probes + 1], text[probes + 1:probes + 2]
            in_c = (iota((cols, slots), 0).astype(F32) == c).astype(F32).astype(BF16)
            return times(jnp.where(r == float(row), text, 0.0), in_c, NT)

        beside = side(0, cols - 1, PAD_C - 1) + side(1, 0, 0)
        above_obs = end(2, rows - 1)
        below_obs = end(3, 0)

        relay(1, 1)
        relay(0, 1)

        for copy in coef_copies:
            copy.wait_recv()
        right = lane[0:8] < 64
        below = iota((8, 128), 0) < 4
        from_left, from_right = col_recv[0], col_recv[1]
        for i in range(3):
            for a in range(tiles):
                coef[i, 8 * a:8 * a + 8, c_out] = jnp.where(
                    right, pltpu.roll(from_right, (256 - 3 * i - a * GROUP) % 128, 1),
                    pltpu.roll(from_left, (256 + 125 - 3 * i - a * GROUP) % 128, 1))
            top, bottom = row_recv[1], row_recv[0]
            first, second = (0, 2, 5)[i], (0, 2, 5)[i] + (2, 3, 2)[i]
            top, bottom = (pltpu.roll(t, s % 8, 0) if s % 8 else t for t, s in ((top, 8 - first), (bottom, 8 - second)))
            coef[i, r_out, c_in] = jnp.where(iota((8, cols), 0) < 4, top, bottom)
            corner = [[pltpu.roll(diag_recv[n, m], (256 + 125 * (1 - m) - 3 * i) % 128, 1) for m in range(2)]
                      for n in range(2)]
            coef[i, r_out, c_out] = jnp.where(
                below, jnp.where(right, corner[1][1], corner[1][0]), jnp.where(right, corner[0][1], corner[0][0]))
        damp, cx, cy = coef[0], coef[1], coef[2]
        cxu, cyl = pltpu.roll(cx, 1, 0), pltpu.roll(cy, 1, 1)
        up_v[...] = cxu
        left_v[...] = cyl
        diag_v[...] = damp + cx + cxu + cy + cyl

        def operator(field):
            return (diag_v[...] * field - coef[1] * pltpu.roll(field, ext_r - 1, 0) - up_v[...] * pltpu.roll(field, 1, 0)
                    - coef[2] * pltpu.roll(field, ext_c - 1, 1) - left_v[...] * pltpu.roll(field, 1, 1))

        for k in range(probes):
            once[k] = operator(prob[k])

        for k in range(probes):
            mine = slice(k * rows, (k + 1) * rows)
            image[k] = operator(once[k])
            inner = image[k, r_in, c_in] + own[mine]
            image[k, r_in, c_in] = inner
            inner_v[k] = inner
            image[k, r_in, c_out] = image[k, r_in, c_out] + beside[mine]
            image[k, ext_r - 1:ext_r, c_in] = image[k, ext_r - 1:ext_r, c_in] + above_obs[k:k + 1]
            image[k, rows:rows + 1, c_in] = image[k, rows:rows + 1, c_in] + below_obs[k:k + 1]
        saves.append(pltpu.make_async_copy(inner_v, image_h, local_sem.at[7]))
        saves[1].start()

        relay(0, 2)

        def fold(x):
            total = jnp.sum(x.reshape(rows // 8, 8, cols), axis=0)
            total = sum(total[:, n * 128:(n + 1) * 128] for n in range(cols // 128))
            return jnp.sum(total, axis=0, keepdims=True)

        block = jnp.concatenate([image[k, r_in, c_in] for k in range(probes)], axis=0)
        picked = times(block, in_col)
        seen = [jnp.sum(picked[k * rows:(k + 1) * rows] * in_row, axis=0, keepdims=True) for k in range(probes)]
        seen = jnp.concatenate(seen + [jnp.zeros((8 - probes, slots), F32)], axis=0)
        seen = jnp.where(keep, seen, 0.0)
        answer = weigh(seen)
        quad = seen * answer
        quad = sum(quad[:, n * 128:(n + 1) * 128] for n in range(slots // 128))
        firsts, seconds, thirds = [], [], []
        for k in range(probes):
            field = image[k]
            inner = field[r_in, c_in]
            firsts.append(fold(prob[k, r_in, c_in] * inner))
            seconds.append(fold(inner * inner))
            twice = operator(field)[r_in, c_in]
            thirds.append(fold(twice * twice) + quad[k:k + 1])
        lines = jnp.concatenate(firsts + seconds + thirds + [jnp.zeros((16 - 3 * probes, 128), F32)], axis=0)
        sums = jnp.sum(lines, axis=1, keepdims=True)
        total = jnp.sum(jnp.where(iota((16, 128), 0) == iota((16, 128), 1), sums, 0.0), axis=0, keepdims=True)

        for stage, (size, got, ssem, rsem) in enumerate(((by, got_y, y_send, y_recv), (bx, got_x, x_send, x_recv))):
            heard(1 - stage, 2 + stage)
            part[stage] = total
            copies = [
                send(part.at[stage], got.at[d - 1], ssem.at[d - 1], rsem.at[d - 1], *((0, d) if stage == 0 else (d, 0)))
                for d in range(1, size)
            ]
            for d, copy in enumerate(copies):
                copy.wait_recv()
                total = total + got[d]
        total_ref[...] = total
        for save in saves:
            save.wait()
        for copy in sends:
            copy.wait_send()

    def finish(total_ref, image_ref, prob_ref, sol_ref, trace_ref):
        total = total_ref[...]
        lane = iota((1, 128), 1)
        m1 = jnp.where(lane < probes, total, 1.0)
        m2 = jnp.where(lane < probes, pltpu.roll(total, 128 - probes, 1), 1.0)
        m3 = jnp.where(lane < probes, pltpu.roll(total, 128 - 2 * probes, 1), 1.0)
        norm0 = float(nx * ny)
        alpha0 = norm0 / m1
        norm1 = alpha0 * alpha0 * m2 - norm0
        alpha1 = norm1 / (alpha0 * alpha0 * (m3 - m2 * m2 / m1))
        on_probe = alpha0 + alpha1 * (1.0 + norm1 / norm0)
        on_image = alpha1 * alpha0
        trace_ref[0, 0] = jnp.sum(jnp.where(lane < probes, alpha0 * norm0 + alpha1 * norm1, 0.0)) / probes
        for k in range(probes):
            sol_ref[k] = on_probe[0, k] * prob_ref[k] - on_image[0, k] * image_ref[k]

    return body, finish, ext_r, ext_c


def solution(mesh):
    bx, by = mesh.shape["gx"], mesh.shape["gy"]

    def per_device(probe_seeds, damping, coupling_x, coupling_y, sensor_count, sensor_cells, obs_weight):
        probes = probe_seeds.shape[0]
        rows, cols = damping.shape
        slots = sensor_cells.shape[-1]
        body, finish, ext_r, ext_c = kernel_of(probes, bx, by, rows, cols)
        dma = pltpu.SemaphoreType.DMA
        plane = pltpu.VMEM((ext_r, ext_c), F32)
        fields = pltpu.VMEM((probes, ext_r, ext_c), F32)
        in_vmem = pl.BlockSpec(memory_space=pltpu.VMEM)
        in_hbm = pl.BlockSpec(memory_space=pltpu.HBM)
        in_smem = pl.BlockSpec(memory_space=pltpu.SMEM)
        field = jax.ShapeDtypeStruct((probes, rows, cols), F32)
        image, prob, total = pl.pallas_call(
            body,
            name="two_steps",
            out_shape=(field, field, jax.ShapeDtypeStruct((1, 128), F32)),
            in_specs=[in_hbm] * 4 + [in_smem] + [in_hbm] * 2,
            out_specs=(pl.BlockSpec(memory_space=pl.ANY), pl.BlockSpec(memory_space=pl.ANY), in_vmem),
            scratch_shapes=[
                pltpu.SMEM((1, probes), jnp.int32),
                pltpu.VMEM((1, slots), jnp.int32), pltpu.VMEM((slots, slots), F32),
                pltpu.VMEM((3, ext_r, ext_c), F32), plane, plane, plane, fields, fields, fields,
                pltpu.VMEM((probes, rows, cols), F32),
                pltpu.VMEM((2, rows, 128), F32), pltpu.VMEM((2, 8, 128), F32),
                pltpu.VMEM((2, 8, cols), F32), pltpu.VMEM((2, 8, cols), F32), pltpu.VMEM((2, 8, 128), F32), pltpu.VMEM((2, 2, 8, 128), F32),
                pltpu.VMEM((8, slots), F32), pltpu.VMEM((4, 8, slots), F32),
                pltpu.VMEM((2, 1, 128), F32), pltpu.VMEM((by - 1, 1, 128), F32), pltpu.VMEM((bx - 1, 1, 128), F32),
                dma((8,)), pltpu.SemaphoreType.REGULAR((2, 4, 2)), dma((8,)), dma((8,)), dma((4,)), dma((4,)),
                dma((by - 1,)), dma((by - 1,)), dma((bx - 1,)), dma((bx - 1,)),
            ],
            compiler_params=pltpu.CompilerParams(
                collective_id=0, has_side_effects=True, vmem_limit_bytes=16 * 2**20),
        )(hbm(probe_seeds.reshape(1, probes)), hbm(damping), hbm(coupling_x), hbm(coupling_y), sensor_count,
          hbm(sensor_cells.reshape(1, slots)), hbm(obs_weight.reshape(slots, slots)))
        sol, trace = pl.pallas_call(
            finish,
            name="finish",
            out_shape=(field, jax.ShapeDtypeStruct((1, 1), F32)),
            in_specs=[in_vmem] * 3,
            out_specs=(in_vmem, in_smem),
            compiler_params=pltpu.CompilerParams(vmem_limit_bytes=16 * 2**20),
        )(total, image, prob)
        return sol, trace.reshape(())

    return jax.shard_map(
        per_device,
        mesh=mesh,
        in_specs=(P(), P("gx", "gy"), P("gx", "gy"), P("gx", "gy"), P("gx", "gy"),
                  P("gx", "gy", None), P("gx", "gy", None, None)),
        out_specs=(P(None, "gx", "gy"), P()),
        check_vma=False,
    )
```

```python
import jax
import jax.numpy as jnp
from jax import lax
from jax.experimental import pallas as pl
from jax.experimental.pallas import tpu as pltpu
from jax.sharding import PartitionSpec as P

MESH = pl.DeviceIdType.MESH
NT = (((1,), (1,)), ((), ()))
F32 = jnp.float32
BF16 = jnp.bfloat16

PAD_R, PAD_C = 8, 128
GROUP = 16


def mix(base):
    mixed = (base ^ ((base >> 16) & 65535)) * 73244475
    mixed = (mixed ^ ((mixed >> 16) & 65535)) * 73244475
    mixed = mixed ^ ((mixed >> 16) & 65535)
    return (2 * ((mixed >> 7) & 1) - 1).astype(F32)


def position(rows, cols):
    return rows * 374761393 + cols * 1103515245


def iota(shape, dim):
    return lax.broadcasted_iota(jnp.int32, shape, dim)


def split3(x):
    high = x.astype(BF16)
    rest = x - high.astype(F32)
    mid = rest.astype(BF16)
    low = (rest - mid.astype(F32)).astype(BF16)
    return high, mid, low


def times(x, y, dims=(((1,), (0,)), ((), ()))):
    total = None
    for part in reversed(split3(x)):
        one = lax.dot_general(part, y, dims, preferred_element_type=F32)
        total = one if total is None else total + one
    return total


def hbm(x):
    return pltpu.with_memory_space_constraint(x, pltpu.HBM)


def kernel_of(probes, bx, by, rows, cols):
    ext_r, ext_c = rows + PAD_R, cols + PAD_C
    nx, ny = bx * rows, by * cols
    r_in, c_in = slice(0, rows), slice(0, cols)
    r_out, c_out = slice(rows, ext_r), slice(cols, ext_c)
    tiles = rows // 8
    cross = [(0, 1), (0, -1), (1, 0), (-1, 0)]
    corners = [(a, b) for a in (-1, 1) for b in (-1, 1)]

    def body(seeds_h, damp_h, cx_h, cy_h, count_s, cells_h, weight_h, image_h, prob_h, total_ref,
             seeds_s, cells_v, weight_v, coef, up_v, left_v, diag_v, prob, once, image, inner_v,
             edge_v, col_send, row_send, row_recv, col_recv, diag_recv, w_send, w_recv, part, got_y, got_x,
             local_sem, known_sem, coef_send, coef_recv, obs_send, obs_recv, y_send, y_recv, x_send, x_recv):
        gx, gy = lax.axis_index("gx"), lax.axis_index("gy")

        def at(dx, dy):
            return (lax.rem(gx + (dx + bx), bx), lax.rem(gy + (dy + by), by))

        barrier = pltpu.get_barrier_semaphore()
        nearest = [(0, 1), (0, by - 1), (1, 0), (bx - 1, 0)] + corners
        for dx, dy in nearest:
            pl.semaphore_signal(barrier, inc=1, device_id=at(dx, dy), device_id_type=MESH)

        loads = [
            pltpu.make_async_copy(damp_h, coef.at[0, r_in, c_in], local_sem.at[0]),
            pltpu.make_async_copy(cx_h, coef.at[1, r_in, c_in], local_sem.at[1]),
            pltpu.make_async_copy(cy_h, coef.at[2, r_in, c_in], local_sem.at[2]),
            pltpu.make_async_copy(cells_h, cells_v, local_sem.at[3]),
            pltpu.make_async_copy(seeds_h, seeds_s, local_sem.at[4]),
            pltpu.make_async_copy(weight_h, weight_v, local_sem.at[5]),
        ]
        for load in loads:
            load.start()
        for load in loads[:3]:
            load.wait()

        lane = iota((rows, 128), 1)
        for n, (start, base) in enumerate(((cols - 128, 3), (0, 0))):
            d, x, y = (coef[i, r_in, start:start + 128] for i in range(3))
            d = pltpu.roll(d, base, 1) if base else d
            edge = jnp.where(lane < 3, d, jnp.where(lane < 6, pltpu.roll(x, base + 3, 1), pltpu.roll(y, base + 6, 1)))
            edge_v[n] = edge
            tile = edge[0:8]
            for a in range(1, tiles):
                tile = jnp.where(lane[0:8] < a * GROUP, tile, pltpu.roll(edge[8 * a:8 * a + 8], a * GROUP, 1))
            col_send[n] = tile
        for n, base in enumerate((rows - 3, 0)):
            row_send[n, 0:2] = coef[0, base + 1 - n:base + 3 - n, c_in]
            row_send[n, 2:5] = coef[1, base:base + 3, c_in]
            row_send[n, 5:7] = coef[2, base + 1 - n:base + 3 - n, c_in]
            row_send[n, 7:8] = coef[2, base:base + 1, c_in]
        for load in loads[3:5]:
            load.wait()
        slots = cells_v.shape[1]
        cell = cells_v[...]
        sensor_r = lax.div(cell, cols)
        sensor_c = lax.rem(cell, cols)
        sub = iota((8, slots), 0)
        seed = jnp.where(sub == 0, seeds_s[0, 0], 0)
        for k in range(1, probes):
            seed = jnp.where(sub == k, seeds_s[0, k], seed)
        live = iota((8, slots), 1) < count_s[0, 0]
        keep = jnp.logical_and(live, sub < probes)
        sampled = mix(seed * 668265261 + position(gx * rows + sensor_r, gy * cols + sensor_c))
        sampled = jnp.where(keep, sampled, 0.0)
        loads[5].wait()
        weight = split3(weight_v[...])

        def weigh(x):
            high, mid, low = split3(x)
            parts = (jnp.concatenate([high, mid, low], axis=0), jnp.concatenate([high, mid], axis=0), high)
            done = [jnp.dot(x_part, w_part, preferred_element_type=F32) for x_part, w_part in zip(parts, weight)]
            return ((done[0][16:24] + done[1][8:16] + done[2]) + (done[0][8:16] + done[1][0:8])) + done[0][0:8]

        exact = sampled.astype(BF16)
        weighted = sum(jnp.dot(exact, part, preferred_element_type=F32) for part in reversed(weight))
        weighted = jnp.where(keep, weighted, 0.0)
        row_f, col_f = sensor_r.astype(F32), sensor_c.astype(F32)
        message = jnp.where(sub == probes, jnp.broadcast_to(row_f, (8, slots)), weighted)
        message = jnp.where(sub == probes + 1, jnp.broadcast_to(col_f, (8, slots)), message)
        w_send[...] = message

        pl.semaphore_wait(barrier, len(nearest))

        assert (bx, by) == (32, 16)

        def hail(axis, step):
            for m, d in enumerate((2**step, -2**step)):
                pl.semaphore_signal(known_sem.at[axis, step, m], inc=1, device_id=at(*((d, 0), (0, d))[axis]),
                                    device_id_type=MESH)

        def heard(axis, step):
            for m in range(2):
                pl.semaphore_wait(known_sem.at[axis, step, m], 1)

        def relay(axis, step):
            heard(axis, step)
            hail(axis, step + 1)

        hail(0, 0)
        hail(1, 0)

        sends = []

        def send(src, dst, ssem, rsem, dx, dy):
            copy = pltpu.make_async_remote_copy(
                src_ref=src, dst_ref=dst, send_sem=ssem, recv_sem=rsem,
                device_id=at(dx, dy), device_id_type=MESH)
            copy.start()
            sends.append(copy)
            return copy

        obs_copies = [
            send(w_send, w_recv.at[n], obs_send.at[n], obs_recv.at[n], dx, dy) for n, (dx, dy) in enumerate(cross)
        ]
        coef_copies = [
            send(edge_v.at[m, rows - 8:rows] if n == 0 else edge_v.at[m, 0:8], diag_recv.at[n, m],
                 coef_send.at[4 + 2 * n + m], coef_recv.at[4 + 2 * n + m], 1 - 2 * n, 1 - 2 * m)
            for n in range(2) for m in range(2)
        ] + [
            send(row_send.at[n], row_recv.at[n], coef_send.at[2 + n], coef_recv.at[2 + n], 1 - 2 * n, 0)
            for n in range(2)
        ] + [
            send(col_send.at[n], col_recv.at[n], coef_send.at[n], coef_recv.at[n], 0, 1 - 2 * n) for n in range(2)
        ]

        row_ids, col_ids = iota((ext_r, ext_c), 0), iota((ext_r, ext_c), 1)
        row_ids = jnp.where(row_ids < rows + PAD_R // 2, row_ids, row_ids - ext_r)
        col_ids = jnp.where(col_ids < cols + PAD_C // 2, col_ids, col_ids - ext_c)
        place = position((gx * rows + row_ids) & (nx - 1), (gy * cols + col_ids) & (ny - 1))
        for k in range(probes):
            prob[k] = mix(seeds_s[0, k] * 668265261 + place)
        saves = [pltpu.make_async_copy(prob.at[:, r_in, c_in], prob_h, local_sem.at[6])]
        saves[0].start()

        in_row = (iota((rows, slots), 0) == sensor_r).astype(F32)
        in_col = (iota((cols, slots), 0) == sensor_c).astype(F32).astype(BF16)
        spread = jnp.concatenate([in_row * weighted[k:k + 1] for k in range(probes)], axis=0)
        own = times(spread, in_col, NT)

        relay(1, 0)
        relay(0, 0)

        for copy in obs_copies:
            copy.wait_recv()

        def side(n, column, at_lane):
            text = w_recv[n]
            r, c = text[probes:probes + 1], text[probes + 1:probes + 2]
            hit = jnp.logical_and(c == float(column), iota((PAD_C, slots), 0) == at_lane)
            in_r = (iota((rows, slots), 0).astype(F32) == r).astype(F32)
            lhs = jnp.concatenate([in_r * text[k:k + 1] for k in range(probes)], axis=0)
            return times(lhs, hit.astype(F32).astype(BF16), NT)

        def end(n, row):
            text = w_recv[n]
            r, c = text[probes:probes + 1], text[probes + 1:probes + 2]
            in_c = (iota((cols, slots), 0).astype(F32) == c).astype(F32).astype(BF16)
            return times(jnp.where(r == float(row), text, 0.0), in_c, NT)

        beside = side(0, cols - 1, PAD_C - 1) + side(1, 0, 0)
        above_obs = end(2, rows - 1)
        below_obs = end(3, 0)

        relay(1, 1)
        relay(0, 1)

        for copy in coef_copies:
            copy.wait_recv()
        right = lane[0:8] < 64
        below = iota((8, 128), 0) < 4
        from_left, from_right = col_recv[0], col_recv[1]
        for i in range(3):
            for a in range(tiles):
                coef[i, 8 * a:8 * a + 8, c_out] = jnp.where(
                    right, pltpu.roll(from_right, (256 - 3 * i - a * GROUP) % 128, 1),
                    pltpu.roll(from_left, (256 + 125 - 3 * i - a * GROUP) % 128, 1))
            top, bottom = row_recv[1], row_recv[0]
            first, second = (0, 2, 5)[i], (0, 2, 5)[i] + (2, 3, 2)[i]
            top, bottom = (pltpu.roll(t, s % 8, 0) if s % 8 else t for t, s in ((top, 8 - first), (bottom, 8 - second)))
            coef[i, r_out, c_in] = jnp.where(iota((8, cols), 0) < 4, top, bottom)
            corner = [[pltpu.roll(diag_recv[n, m], (256 + 125 * (1 - m) - 3 * i) % 128, 1) for m in range(2)]
                      for n in range(2)]
            coef[i, r_out, c_out] = jnp.where(
                below, jnp.where(right, corner[1][1], corner[1][0]), jnp.where(right, corner[0][1], corner[0][0]))
        damp, cx, cy = coef[0], coef[1], coef[2]
        cxu, cyl = pltpu.roll(cx, 1, 0), pltpu.roll(cy, 1, 1)
        up_v[...] = cxu
        left_v[...] = cyl
        diag_v[...] = damp + cx + cxu + cy + cyl

        def operator(field):
            return (diag_v[...] * field - coef[1] * pltpu.roll(field, ext_r - 1, 0) - up_v[...] * pltpu.roll(field, 1, 0)
                    - coef[2] * pltpu.roll(field, ext_c - 1, 1) - left_v[...] * pltpu.roll(field, 1, 1))

        for k in range(probes):
            once[k] = operator(prob[k])

        for k in range(probes):
            mine = slice(k * rows, (k + 1) * rows)
            image[k] = operator(once[k])
            inner = image[k, r_in, c_in] + own[mine]
            image[k, r_in, c_in] = inner
            inner_v[k] = inner
            image[k, r_in, c_out] = image[k, r_in, c_out] + beside[mine]
            image[k, ext_r - 1:ext_r, c_in] = image[k, ext_r - 1:ext_r, c_in] + above_obs[k:k + 1]
            image[k, rows:rows + 1, c_in] = image[k, rows:rows + 1, c_in] + below_obs[k:k + 1]
        saves.append(pltpu.make_async_copy(inner_v, image_h, local_sem.at[7]))
        saves[1].start()

        relay(0, 2)

        def fold(x):
            total = jnp.sum(x.reshape(rows // 8, 8, cols), axis=0)
            total = sum(total[:, n * 128:(n + 1) * 128] for n in range(cols // 128))
            return jnp.sum(total, axis=0, keepdims=True)

        block = jnp.concatenate([image[k, r_in, c_in] for k in range(probes)], axis=0)
        picked = times(block, in_col)
        seen = [jnp.sum(picked[k * rows:(k + 1) * rows] * in_row, axis=0, keepdims=True) for k in range(probes)]
        seen = jnp.concatenate(seen + [jnp.zeros((8 - probes, slots), F32)], axis=0)
        seen = jnp.where(keep, seen, 0.0)
        answer = weigh(seen)
        quad = seen * answer
        quad = sum(quad[:, n * 128:(n + 1) * 128] for n in range(slots // 128))
        firsts, seconds, thirds = [], [], []
        for k in range(probes):
            field = image[k]
            inner = field[r_in, c_in]
            firsts.append(fold(prob[k, r_in, c_in] * inner))
            seconds.append(fold(inner * inner))
            twice = operator(field)[r_in, c_in]
            thirds.append(fold(twice * twice) + quad[k:k + 1])
        lines = jnp.concatenate(firsts + seconds + thirds + [jnp.zeros((16 - 3 * probes, 128), F32)], axis=0)
        sums = jnp.sum(lines, axis=1, keepdims=True)
        total = jnp.sum(jnp.where(iota((16, 128), 0) == iota((16, 128), 1), sums, 0.0), axis=0, keepdims=True)

        for stage, (size, got, ssem, rsem) in enumerate(((by, got_y, y_send, y_recv), (bx, got_x, x_send, x_recv))):
            heard(1 - stage, 2 + stage)
            part[stage] = total
            copies = [
                send(part.at[stage], got.at[d - 1], ssem.at[d - 1], rsem.at[d - 1], *((0, d) if stage == 0 else (d, 0)))
                for d in range(1, size)
            ]
            for copy in copies:
                copy.wait_recv()
            lines = [total] + [got[d] for d in range(size - 1)]
            while len(lines) > 1:
                lines = [lines[n] + lines[n + 1] for n in range(0, len(lines), 2)]
            total = lines[0]
        total_ref[...] = total
        for save in saves:
            save.wait()
        for copy in sends:
            copy.wait_send()

    def finish(total_ref, image_ref, prob_ref, sol_ref, trace_ref):
        total = total_ref[...]
        lane = iota((1, 128), 1)
        m1 = jnp.where(lane < probes, total, 1.0)
        m2 = jnp.where(lane < probes, pltpu.roll(total, 128 - probes, 1), 1.0)
        m3 = jnp.where(lane < probes, pltpu.roll(total, 128 - 2 * probes, 1), 1.0)
        norm0 = float(nx * ny)
        alpha0 = norm0 / m1
        norm1 = alpha0 * alpha0 * m2 - norm0
        alpha1 = norm1 / (alpha0 * alpha0 * (m3 - m2 * m2 / m1))
        on_probe = alpha0 + alpha1 * (1.0 + norm1 / norm0)
        on_image = alpha1 * alpha0
        trace_ref[0, 0] = jnp.sum(jnp.where(lane < probes, alpha0 * norm0 + alpha1 * norm1, 0.0)) / probes
        for k in range(probes):
            sol_ref[k] = on_probe[0, k] * prob_ref[k] - on_image[0, k] * image_ref[k]

    return body, finish, ext_r, ext_c


def solution(mesh):
    bx, by = mesh.shape["gx"], mesh.shape["gy"]

    def per_device(probe_seeds, damping, coupling_x, coupling_y, sensor_count, sensor_cells, obs_weight):
        probes = probe_seeds.shape[0]
        rows, cols = damping.shape
        slots = sensor_cells.shape[-1]
        body, finish, ext_r, ext_c = kernel_of(probes, bx, by, rows, cols)
        dma = pltpu.SemaphoreType.DMA
        plane = pltpu.VMEM((ext_r, ext_c), F32)
        fields = pltpu.VMEM((probes, ext_r, ext_c), F32)
        in_vmem = pl.BlockSpec(memory_space=pltpu.VMEM)
        in_hbm = pl.BlockSpec(memory_space=pltpu.HBM)
        in_smem = pl.BlockSpec(memory_space=pltpu.SMEM)
        field = jax.ShapeDtypeStruct((probes, rows, cols), F32)
        image, prob, total = pl.pallas_call(
            body,
            name="two_steps",
            out_shape=(field, field, jax.ShapeDtypeStruct((1, 128), F32)),
            in_specs=[in_hbm] * 4 + [in_smem] + [in_hbm] * 2,
            out_specs=(pl.BlockSpec(memory_space=pl.ANY), pl.BlockSpec(memory_space=pl.ANY), in_vmem),
            scratch_shapes=[
                pltpu.SMEM((1, probes), jnp.int32),
                pltpu.VMEM((1, slots), jnp.int32), pltpu.VMEM((slots, slots), F32),
                pltpu.VMEM((3, ext_r, ext_c), F32), plane, plane, plane, fields, fields, fields,
                pltpu.VMEM((probes, rows, cols), F32),
                pltpu.VMEM((2, rows, 128), F32), pltpu.VMEM((2, 8, 128), F32),
                pltpu.VMEM((2, 8, cols), F32), pltpu.VMEM((2, 8, cols), F32), pltpu.VMEM((2, 8, 128), F32), pltpu.VMEM((2, 2, 8, 128), F32),
                pltpu.VMEM((8, slots), F32), pltpu.VMEM((4, 8, slots), F32),
                pltpu.VMEM((2, 1, 128), F32), pltpu.VMEM((by - 1, 1, 128), F32), pltpu.VMEM((bx - 1, 1, 128), F32),
                dma((8,)), pltpu.SemaphoreType.REGULAR((2, 4, 2)), dma((8,)), dma((8,)), dma((4,)), dma((4,)),
                dma((by - 1,)), dma((by - 1,)), dma((bx - 1,)), dma((bx - 1,)),
            ],
            compiler_params=pltpu.CompilerParams(
                collective_id=0, has_side_effects=True, vmem_limit_bytes=16 * 2**20),
        )(hbm(probe_seeds.reshape(1, probes)), hbm(damping), hbm(coupling_x), hbm(coupling_y), sensor_count,
          hbm(sensor_cells.reshape(1, slots)), hbm(obs_weight.reshape(slots, slots)))
        sol, trace = pl.pallas_call(
            finish,
            name="finish",
            out_shape=(field, jax.ShapeDtypeStruct((1, 1), F32)),
            in_specs=[in_vmem] * 3,
            out_specs=(in_vmem, in_smem),
            compiler_params=pltpu.CompilerParams(vmem_limit_bytes=16 * 2**20),
        )(total, image, prob)
        return sol, trace.reshape(())

    return jax.shard_map(
        per_device,
        mesh=mesh,
        in_specs=(P(), P("gx", "gy"), P("gx", "gy"), P("gx", "gy"), P("gx", "gy"),
                  P("gx", "gy", None), P("gx", "gy", None, None)),
        out_specs=(P(None, "gx", "gy"), P()),
        check_vma=False,
    )
```

```python
import jax
import jax.numpy as jnp
from jax import lax
from jax.experimental import pallas as pl
from jax.experimental.pallas import tpu as pltpu
from jax.sharding import PartitionSpec as P

MESH = pl.DeviceIdType.MESH
NT = (((1,), (1,)), ((), ()))
F32 = jnp.float32
BF16 = jnp.bfloat16

PAD_R, PAD_C = 8, 128
GROUP = 16


def mix(base):
    mixed = (base ^ ((base >> 16) & 65535)) * 73244475
    mixed = (mixed ^ ((mixed >> 16) & 65535)) * 73244475
    mixed = mixed ^ ((mixed >> 16) & 65535)
    return (2 * ((mixed >> 7) & 1) - 1).astype(F32)


def position(rows, cols):
    return rows * 374761393 + cols * 1103515245


def iota(shape, dim):
    return lax.broadcasted_iota(jnp.int32, shape, dim)


def split3(x):
    high = x.astype(BF16)
    rest = x - high.astype(F32)
    mid = rest.astype(BF16)
    low = (rest - mid.astype(F32)).astype(BF16)
    return high, mid, low


def times(x, y, dims=(((1,), (0,)), ((), ()))):
    total = None
    for part in reversed(split3(x)):
        one = lax.dot_general(part, y, dims, preferred_element_type=F32)
        total = one if total is None else total + one
    return total


def hbm(x):
    return pltpu.with_memory_space_constraint(x, pltpu.HBM)


def kernel_of(probes, bx, by, rows, cols):
    ext_r, ext_c = rows + PAD_R, cols + PAD_C
    nx, ny = bx * rows, by * cols
    r_in, c_in = slice(0, rows), slice(0, cols)
    r_out, c_out = slice(rows, ext_r), slice(cols, ext_c)
    tiles = rows // 8
    cross = [(0, 1), (0, -1), (1, 0), (-1, 0)]
    corners = [(a, b) for a in (-1, 1) for b in (-1, 1)]

    def body(seeds_h, damp_h, cx_h, cy_h, count_s, cells_h, weight_h, image_h, prob_h, total_ref,
             seeds_s, cells_v, weight_v, coef, up_v, left_v, diag_v, prob, once, image, inner_v,
             edge_v, col_send, row_send, row_recv, col_recv, diag_recv, w_send, w_recv, part, got_y, got_x,
             local_sem, known_sem, coef_send, coef_recv, obs_send, obs_recv, y_send, y_recv, x_send, x_recv):
        gx, gy = lax.axis_index("gx"), lax.axis_index("gy")

        def at(dx, dy):
            return (lax.rem(gx + (dx + bx), bx), lax.rem(gy + (dy + by), by))

        barrier = pltpu.get_barrier_semaphore()
        nearest = [(0, 1), (0, by - 1), (1, 0), (bx - 1, 0)] + corners
        for dx, dy in nearest:
            pl.semaphore_signal(barrier, inc=1, device_id=at(dx, dy), device_id_type=MESH)

        loads = [
            pltpu.make_async_copy(damp_h, coef.at[0, r_in, c_in], local_sem.at[0]),
            pltpu.make_async_copy(cx_h, coef.at[1, r_in, c_in], local_sem.at[1]),
            pltpu.make_async_copy(cy_h, coef.at[2, r_in, c_in], local_sem.at[2]),
            pltpu.make_async_copy(cells_h, cells_v, local_sem.at[3]),
            pltpu.make_async_copy(seeds_h, seeds_s, local_sem.at[4]),
            pltpu.make_async_copy(weight_h, weight_v, local_sem.at[5]),
        ]
        for load in loads:
            load.start()
        for load in loads[:3]:
            load.wait()

        lane = iota((rows, 128), 1)
        for n, (start, base) in enumerate(((cols - 128, 3), (0, 0))):
            d, x, y = (coef[i, r_in, start:start + 128] for i in range(3))
            d = pltpu.roll(d, base, 1) if base else d
            edge = jnp.where(lane < 3, d, jnp.where(lane < 6, pltpu.roll(x, base + 3, 1), pltpu.roll(y, base + 6, 1)))
            edge_v[n] = edge
            tile = edge[0:8]
            for a in range(1, tiles):
                tile = jnp.where(lane[0:8] < a * GROUP, tile, pltpu.roll(edge[8 * a:8 * a + 8], a * GROUP, 1))
            col_send[n] = tile
        for n, base in enumerate((rows - 3, 0)):
            row_send[n, 0:2] = coef[0, base + 1 - n:base + 3 - n, c_in]
            row_send[n, 2:5] = coef[1, base:base + 3, c_in]
            row_send[n, 5:7] = coef[2, base + 1 - n:base + 3 - n, c_in]
            row_send[n, 7:8] = coef[2, base:base + 1, c_in]
        for load in loads[3:5]:
            load.wait()
        slots = cells_v.shape[1]
        cell = cells_v[...]
        sensor_r = lax.div(cell, cols)
        sensor_c = lax.rem(cell, cols)
        sub = iota((8, slots), 0)
        seed = jnp.where(sub == 0, seeds_s[0, 0], 0)
        for k in range(1, probes):
            seed = jnp.where(sub == k, seeds_s[0, k], seed)
        live = iota((8, slots), 1) < count_s[0, 0]
        keep = jnp.logical_and(live, sub < probes)
        sampled = mix(seed * 668265261 + position(gx * rows + sensor_r, gy * cols + sensor_c))
        sampled = jnp.where(keep, sampled, 0.0)
        loads[5].wait()
        weight = split3(weight_v[...])

        def weigh(x):
            high, mid, low = split3(x)
            parts = (jnp.concatenate([high, mid, low], axis=0), jnp.concatenate([high, mid], axis=0), high)
            done = [jnp.dot(x_part, w_part, preferred_element_type=F32) for x_part, w_part in zip(parts, weight)]
            return ((done[0][16:24] + done[1][8:16] + done[2]) + (done[0][8:16] + done[1][0:8])) + done[0][0:8]

        exact = sampled.astype(BF16)
        weighted = sum(jnp.dot(exact, part, preferred_element_type=F32) for part in reversed(weight))
        weighted = jnp.where(keep, weighted, 0.0)
        row_f, col_f = sensor_r.astype(F32), sensor_c.astype(F32)
        message = jnp.where(sub == probes, jnp.broadcast_to(row_f, (8, slots)), weighted)
        message = jnp.where(sub == probes + 1, jnp.broadcast_to(col_f, (8, slots)), message)
        w_send[...] = message

        pl.semaphore_wait(barrier, len(nearest))

        assert (bx, by) == (32, 16)

        def hail(axis, step):
            for m, d in enumerate((2**step, -2**step)):
                pl.semaphore_signal(known_sem.at[axis, step, m], inc=1, device_id=at(*((d, 0), (0, d))[axis]),
                                    device_id_type=MESH)

        def heard(axis, step):
            for m in range(2):
                pl.semaphore_wait(known_sem.at[axis, step, m], 1)

        def relay(axis, step):
            heard(axis, step)
            hail(axis, step + 1)

        hail(0, 0)
        hail(1, 0)

        sends = []

        def send(src, dst, ssem, rsem, dx, dy):
            copy = pltpu.make_async_remote_copy(
                src_ref=src, dst_ref=dst, send_sem=ssem, recv_sem=rsem,
                device_id=at(dx, dy), device_id_type=MESH)
            copy.start()
            sends.append(copy)
            return copy

        obs_copies = [
            send(w_send, w_recv.at[n], obs_send.at[n], obs_recv.at[n], dx, dy) for n, (dx, dy) in enumerate(cross)
        ]
        coef_copies = [
            send(edge_v.at[m, rows - 8:rows] if n == 0 else edge_v.at[m, 0:8], diag_recv.at[n, m],
                 coef_send.at[4 + 2 * n + m], coef_recv.at[4 + 2 * n + m], 1 - 2 * n, 1 - 2 * m)
            for n in range(2) for m in range(2)
        ] + [
            send(row_send.at[n], row_recv.at[n], coef_send.at[2 + n], coef_recv.at[2 + n], 1 - 2 * n, 0)
            for n in range(2)
        ] + [
            send(col_send.at[n], col_recv.at[n], coef_send.at[n], coef_recv.at[n], 0, 1 - 2 * n) for n in range(2)
        ]

        row_ids, col_ids = iota((ext_r, ext_c), 0), iota((ext_r, ext_c), 1)
        row_ids = jnp.where(row_ids < rows + PAD_R // 2, row_ids, row_ids - ext_r)
        col_ids = jnp.where(col_ids < cols + PAD_C // 2, col_ids, col_ids - ext_c)
        place = position((gx * rows + row_ids) & (nx - 1), (gy * cols + col_ids) & (ny - 1))
        for k in range(probes):
            prob[k] = mix(seeds_s[0, k] * 668265261 + place)
        saves = [pltpu.make_async_copy(prob.at[:, r_in, c_in], prob_h, local_sem.at[6])]
        saves[0].start()

        in_row = (iota((rows, slots), 0) == sensor_r).astype(F32)
        in_col = (iota((cols, slots), 0) == sensor_c).astype(F32).astype(BF16)
        spread = jnp.concatenate([in_row * weighted[k:k + 1] for k in range(probes)], axis=0)
        own = times(spread, in_col, NT)

        relay(1, 0)
        relay(0, 0)

        for copy in obs_copies:
            copy.wait_recv()

        def side(n, column, at_lane):
            text = w_recv[n]
            r, c = text[probes:probes + 1], text[probes + 1:probes + 2]
            hit = jnp.logical_and(c == float(column), iota((PAD_C, slots), 0) == at_lane)
            in_r = (iota((rows, slots), 0).astype(F32) == r).astype(F32)
            lhs = jnp.concatenate([in_r * text[k:k + 1] for k in range(probes)], axis=0)
            return times(lhs, hit.astype(F32).astype(BF16), NT)

        def end(n, row):
            text = w_recv[n]
            r, c = text[probes:probes + 1], text[probes + 1:probes + 2]
            in_c = (iota((cols, slots), 0).astype(F32) == c).astype(F32).astype(BF16)
            return times(jnp.where(r == float(row), text, 0.0), in_c, NT)

        beside = side(0, cols - 1, PAD_C - 1) + side(1, 0, 0)
        above_obs = end(2, rows - 1)
        below_obs = end(3, 0)

        relay(1, 1)
        relay(0, 1)

        for copy in coef_copies:
            copy.wait_recv()
        right = lane[0:8] < 64
        below = iota((8, 128), 0) < 4
        from_left, from_right = col_recv[0], col_recv[1]
        for i in range(3):
            for a in range(tiles):
                coef[i, 8 * a:8 * a + 8, c_out] = jnp.where(
                    right, pltpu.roll(from_right, (256 - 3 * i - a * GROUP) % 128, 1),
                    pltpu.roll(from_left, (256 + 125 - 3 * i - a * GROUP) % 128, 1))
            top, bottom = row_recv[1], row_recv[0]
            first, second = (0, 2, 5)[i], (0, 2, 5)[i] + (2, 3, 2)[i]
            top, bottom = (pltpu.roll(t, s % 8, 0) if s % 8 else t for t, s in ((top, 8 - first), (bottom, 8 - second)))
            coef[i, r_out, c_in] = jnp.where(iota((8, cols), 0) < 4, top, bottom)
            corner = [[pltpu.roll(diag_recv[n, m], (256 + 125 * (1 - m) - 3 * i) % 128, 1) for m in range(2)]
                      for n in range(2)]
            coef[i, r_out, c_out] = jnp.where(
                below, jnp.where(right, corner[1][1], corner[1][0]), jnp.where(right, corner[0][1], corner[0][0]))
        damp, cx, cy = coef[0], coef[1], coef[2]
        cxu, cyl = pltpu.roll(cx, 1, 0), pltpu.roll(cy, 1, 1)
        up_v[...] = cxu
        left_v[...] = cyl
        diag_v[...] = damp + cx + cxu + cy + cyl

        def operator(field):
            return (diag_v[...] * field - coef[1] * pltpu.roll(field, ext_r - 1, 0) - up_v[...] * pltpu.roll(field, 1, 0)
                    - coef[2] * pltpu.roll(field, ext_c - 1, 1) - left_v[...] * pltpu.roll(field, 1, 1))

        for k in range(probes):
            once[k] = operator(prob[k])

        for k in range(probes):
            mine = slice(k * rows, (k + 1) * rows)
            image[k] = operator(once[k])
            inner = image[k, r_in, c_in] + own[mine]
            image[k, r_in, c_in] = inner
            inner_v[k] = inner
            image[k, r_in, c_out] = image[k, r_in, c_out] + beside[mine]
            image[k, ext_r - 1:ext_r, c_in] = image[k, ext_r - 1:ext_r, c_in] + above_obs[k:k + 1]
            image[k, rows:rows + 1, c_in] = image[k, rows:rows + 1, c_in] + below_obs[k:k + 1]
        saves.append(pltpu.make_async_copy(inner_v, image_h, local_sem.at[7]))
        saves[1].start()

        def fold(x):
            total = jnp.sum(x.reshape(rows // 8, 8, cols), axis=0)
            total = sum(total[:, n * 128:(n + 1) * 128] for n in range(cols // 128))
            return jnp.sum(total, axis=0, keepdims=True)

        block = jnp.concatenate([image[k, r_in, c_in] for k in range(probes)], axis=0)
        picked = times(block, in_col)
        seen = [jnp.sum(picked[k * rows:(k + 1) * rows] * in_row, axis=0, keepdims=True) for k in range(probes)]
        seen = jnp.concatenate(seen + [jnp.zeros((8 - probes, slots), F32)], axis=0)
        seen = jnp.where(keep, seen, 0.0)
        answer = weigh(seen)
        quad = seen * answer
        quad = sum(quad[:, n * 128:(n + 1) * 128] for n in range(slots // 128))
        firsts, seconds, thirds = [], [], []
        for k in range(probes):
            field = image[k]
            inner = field[r_in, c_in]
            firsts.append(fold(prob[k, r_in, c_in] * inner))
            seconds.append(fold(inner * inner))
            twice = operator(field)[r_in, c_in]
            thirds.append(fold(twice * twice) + quad[k:k + 1])
        lines = jnp.concatenate(firsts + seconds + thirds + [jnp.zeros((16 - 3 * probes, 128), F32)], axis=0)
        sums = jnp.sum(lines, axis=1, keepdims=True)
        total = jnp.sum(jnp.where(iota((16, 128), 0) == iota((16, 128), 1), sums, 0.0), axis=0, keepdims=True)

        for stage, (size, got, ssem, rsem) in enumerate(((by, got_y, y_send, y_recv), (bx, got_x, x_send, x_recv))):
            heard(1 - stage, 2 + stage)
            part[stage] = total
            copies = [
                send(part.at[stage], got.at[d - 1], ssem.at[d - 1], rsem.at[d - 1], *((0, d) if stage == 0 else (d, 0)))
                for d in range(1, size)
            ]
            if stage == 0:
                relay(0, 2)
            for copy in copies:
                copy.wait_recv()
            lines = [total] + [got[d] for d in range(size - 1)]
            while len(lines) > 1:
                lines = [lines[n] + lines[n + 1] for n in range(0, len(lines), 2)]
            total = lines[0]
        total_ref[...] = total
        for save in saves:
            save.wait()
        for copy in sends:
            copy.wait_send()

    def finish(total_ref, image_ref, prob_ref, sol_ref, trace_ref):
        total = total_ref[...]
        lane = iota((1, 128), 1)
        m1 = jnp.where(lane < probes, total, 1.0)
        m2 = jnp.where(lane < probes, pltpu.roll(total, 128 - probes, 1), 1.0)
        m3 = jnp.where(lane < probes, pltpu.roll(total, 128 - 2 * probes, 1), 1.0)
        norm0 = float(nx * ny)
        alpha0 = norm0 / m1
        norm1 = alpha0 * alpha0 * m2 - norm0
        alpha1 = norm1 / (alpha0 * alpha0 * (m3 - m2 * m2 / m1))
        on_probe = alpha0 + alpha1 * (1.0 + norm1 / norm0)
        on_image = alpha1 * alpha0
        trace_ref[0, 0] = jnp.sum(jnp.where(lane < probes, alpha0 * norm0 + alpha1 * norm1, 0.0)) / probes
        for k in range(probes):
            sol_ref[k] = on_probe[0, k] * prob_ref[k] - on_image[0, k] * image_ref[k]

    return body, finish, ext_r, ext_c


def solution(mesh):
    bx, by = mesh.shape["gx"], mesh.shape["gy"]

    def per_device(probe_seeds, damping, coupling_x, coupling_y, sensor_count, sensor_cells, obs_weight):
        probes = probe_seeds.shape[0]
        rows, cols = damping.shape
        slots = sensor_cells.shape[-1]
        body, finish, ext_r, ext_c = kernel_of(probes, bx, by, rows, cols)
        dma = pltpu.SemaphoreType.DMA
        plane = pltpu.VMEM((ext_r, ext_c), F32)
        fields = pltpu.VMEM((probes, ext_r, ext_c), F32)
        in_vmem = pl.BlockSpec(memory_space=pltpu.VMEM)
        in_hbm = pl.BlockSpec(memory_space=pltpu.HBM)
        in_smem = pl.BlockSpec(memory_space=pltpu.SMEM)
        field = jax.ShapeDtypeStruct((probes, rows, cols), F32)
        image, prob, total = pl.pallas_call(
            body,
            name="two_steps",
            out_shape=(field, field, jax.ShapeDtypeStruct((1, 128), F32)),
            in_specs=[in_hbm] * 4 + [in_smem] + [in_hbm] * 2,
            out_specs=(pl.BlockSpec(memory_space=pl.ANY), pl.BlockSpec(memory_space=pl.ANY), in_vmem),
            scratch_shapes=[
                pltpu.SMEM((1, probes), jnp.int32),
                pltpu.VMEM((1, slots), jnp.int32), pltpu.VMEM((slots, slots), F32),
                pltpu.VMEM((3, ext_r, ext_c), F32), plane, plane, plane, fields, fields, fields,
                pltpu.VMEM((probes, rows, cols), F32),
                pltpu.VMEM((2, rows, 128), F32), pltpu.VMEM((2, 8, 128), F32),
                pltpu.VMEM((2, 8, cols), F32), pltpu.VMEM((2, 8, cols), F32), pltpu.VMEM((2, 8, 128), F32), pltpu.VMEM((2, 2, 8, 128), F32),
                pltpu.VMEM((8, slots), F32), pltpu.VMEM((4, 8, slots), F32),
                pltpu.VMEM((2, 1, 128), F32), pltpu.VMEM((by - 1, 1, 128), F32), pltpu.VMEM((bx - 1, 1, 128), F32),
                dma((8,)), pltpu.SemaphoreType.REGULAR((2, 4, 2)), dma((8,)), dma((8,)), dma((4,)), dma((4,)),
                dma((by - 1,)), dma((by - 1,)), dma((bx - 1,)), dma((bx - 1,)),
            ],
            compiler_params=pltpu.CompilerParams(
                collective_id=0, has_side_effects=True, vmem_limit_bytes=16 * 2**20),
        )(hbm(probe_seeds.reshape(1, probes)), hbm(damping), hbm(coupling_x), hbm(coupling_y), sensor_count,
          hbm(sensor_cells.reshape(1, slots)), hbm(obs_weight.reshape(slots, slots)))
        sol, trace = pl.pallas_call(
            finish,
            name="finish",
            out_shape=(field, jax.ShapeDtypeStruct((1, 1), F32)),
            in_specs=[in_vmem] * 3,
            out_specs=(in_vmem, in_smem),
            compiler_params=pltpu.CompilerParams(vmem_limit_bytes=16 * 2**20),
        )(total, image, prob)
        return sol, trace.reshape(())

    return jax.shard_map(
        per_device,
        mesh=mesh,
        in_specs=(P(), P("gx", "gy"), P("gx", "gy"), P("gx", "gy"), P("gx", "gy"),
                  P("gx", "gy", None), P("gx", "gy", None, None)),
        out_specs=(P(None, "gx", "gy"), P()),
        check_vma=False,
    )
```
